32 devices in a mesh: groups: 2 (over x), row: 16 (over z, y, core).
Axes of the slice: x: 2, y: 2, z: 4, core: 2. Of those that a mesh axis runs over, the one named last changes fastest.
Arguments:
- factor_panel: bfloat16 [32768, 2048], P(('groups', 'row')), parts along dimension 0, may hold values from -0.25 to 0.25
- pivots: float32 [4096], P('groups'), parts along dimension 0, may hold values from 1 to 1.25
- right_sides: float32 [32768, 256], P(('groups', 'row')), parts along dimension 0, may hold values from -6 to 6
- block_home: int32 [32], replicated, may hold values from 0 to 31, each once
Outputs:
- remainder: float32 [32768, 256], P('groups', 'row'), parts along dimension 0
- psf_variance: float32 [512], P(('groups', 'row')), parts along dimension 0
The draws below stay inside these ranges and needn't reach their ends.
There are 2 independent parts, one for each index of `groups`. The reference program is written for one: setup_inputs(seed, part) draws one part's arguments, and reference() takes and returns one part's arrays. A program takes and returns all parts, laid end to end along the dimension named above; an argument that names none is the same for every part. Nothing has to cross between parts.
Inputs may be any that keep to these rules, and one draw needn't show every extreme that they name: block_home[g] is the stored position of global block g; position p is slot p % 2 of row device p // 2; every position holds exactly one block.
All inputs are finite; a program needn't handle non-finite values.
Results may differ from the reference program's by a relative error of at most 0.0042.
Values may be sent and summed in bfloat16 or wider, within the bound.
No kernel may reach another device: no remote copies, remote signals or barrier semaphores. Data moves between devices by JAX's collectives and lax.ppermute only.
A program may use at most 128 MiB of HBM per device.

```python
import math
import jax
import jax.numpy as jnp
from jax import lax

BLOCK = 512
STEPS = 4
PANEL = 2048
NBLOCKS = 32
ORDER = 16384
RHS = 256


def steps_of(own_key, dims, cuts, smallest, high):
    factor_of, own = 1.0, jax.random.fold_in(own_key, 6)
    for axis_at, shards_of in cuts:
        steps = jnp.exp(jax.random.uniform(jax.random.fold_in(own, axis_at), (shards_of,), jnp.float32, smallest / len(cuts), high / len(cuts)))
        factor_of = factor_of * jnp.repeat(steps, dims[axis_at] // shards_of).reshape([-1 if axis == axis_at else 1 for axis in range(len(dims))])
    return factor_of


def scatter_about(rng, dims, scale, bound, cuts=(), held_as=jnp.bfloat16):
    drawn = scale * jax.random.normal(rng, dims, jnp.float32)
    if cuts:
        drawn = drawn * steps_of(rng, dims, cuts, -0.22, 0.18)
    return jnp.clip(drawn, -bound, bound).astype(held_as)


def setup_inputs(seed: int = 0, part: int = 0) -> dict:
    splits = jax.random.split(jax.random.key(seed), 5)
    part_keys = jax.random.split(jax.random.fold_in(splits[4], part), 5)
    return {
        "factor_panel": scatter_about(part_keys[0], (ORDER, PANEL), BLOCK ** -0.5, 0.25, ((0, 16),)),
        "pivots": jnp.clip(jnp.exp(jax.random.uniform(part_keys[1], (PANEL,), jnp.float32, math.log(1.0), math.log(1.25))), 1.0, 1.25),
        "right_sides": scatter_about(part_keys[2], (ORDER, RHS), 1.0, 6.0, ((0, 16),), jnp.float32),
        "block_home": jax.random.permutation(splits[3], NBLOCKS).astype(jnp.int32),
    }


def reference(factor_panel, pivots, right_sides, block_home):
    factor_blocks = factor_panel.reshape(NBLOCKS, BLOCK, PANEL)[block_home]
    partial_value = right_sides.reshape(NBLOCKS, BLOCK, RHS)[block_home]
    block_index = jnp.arange(NBLOCKS)
    for k in range(STEPS):
        diag_rows = factor_blocks[k][:, k * BLOCK:(k + 1) * BLOCK].astype(jnp.float32)
        diag_block = jnp.tril(diag_rows, -1) + jnp.diag(pivots[k * BLOCK:(k + 1) * BLOCK])
        solution = jax.scipy.linalg.solve_triangular(diag_block, partial_value[k], lower=True).astype(jnp.bfloat16)

        def one_block(rows_block):
            return jnp.dot(rows_block[:, k * BLOCK:(k + 1) * BLOCK].astype(jnp.float32), solution.astype(jnp.float32), preferred_element_type=jnp.float32)
        update = lax.map(one_block, factor_blocks)
        active = (block_index > k).astype(jnp.float32)
        partial_value = partial_value - active[:, None, None] * update
        partial_value = partial_value.at[k].set(solution.astype(jnp.float32))
    remainder = partial_value.reshape(ORDER, RHS)
    solved = remainder[:STEPS * BLOCK]
    psf_variance = jnp.mean(solved * solved, axis=0)
    return (remainder, psf_variance)
```

```python
import functools

import jax
import jax.numpy as jnp
from jax import lax
from jax.experimental import pallas as pl
from jax.experimental.pallas import tpu as pltpu
from jax.sharding import PartitionSpec as P

BLOCK = 512
HALF = 256
STEPS = 4
PANEL = 2048
BF = jnp.bfloat16
F32 = jnp.float32
VMEM_LIMIT = 24 * 1024 * 1024


def mm(a, b):
    return jnp.dot(a, b, preferred_element_type=F32)


def mm_nt(a, b):
    return lax.dot_general(a, b, (((1,), (1,)), ((), ())), preferred_element_type=F32)


def parts(value):
    high = value.astype(BF)
    return high, (value - high.astype(F32)).astype(BF)


def mm3(a_high, a_low, b):
    b_high, b_low = parts(b)
    return mm(a_high, b_high) + (mm(a_high, b_low) + mm(a_low, b_high))


def invert(tiles, pivot_rows):
    shape = tiles[0].shape
    row = lax.broadcasted_iota(jnp.int32, shape, 0)
    col = lax.broadcasted_iota(jnp.int32, shape, 1)
    apart = row ^ col
    lower = row > col
    inverses = []
    for tile, pivot in zip(tiles, pivot_rows):
        across = 1.0 / pivot
        diag = jnp.where(row == col, across, 0.0)
        down = jnp.sum(diag, axis=1, keepdims=True)
        first = jnp.where((apart == 1) & lower, tile.astype(F32), 0.0)
        inverses.append(diag - down * first * across)
    halves = [parts(value) for value in inverses]
    bit = 1
    while (2 << bit) <= shape[0]:
        mask = (lax.shift_right_logical(apart, bit) == 1) & lower
        for at, tile in enumerate(tiles):
            high, low = halves[at]
            link = jnp.where(mask, tile.astype(F32), 0.0).astype(BF)
            inner = mm(link, high) + mm(link, low)
            inverses[at] = inverses[at] - mm3(high, low, inner)
            halves[at] = parts(inverses[at])
        bit += 1
    return halves


def solve(tile_cross, inv, rows):
    (a_high, a_low), (b_high, b_low) = inv
    top = mm3(a_high, a_low, rows[:HALF])
    top_high, top_low = parts(top)
    rest = rows[HALF:] - (mm(tile_cross, top_high) + mm(tile_cross, top_low))
    return top.astype(BF), mm3(b_high, b_low, rest).astype(BF)


def put_halves(core, top, bottom, keep_ref, send_ref):
    first = core == 0
    keep_ref[...] = jnp.where(first, top, bottom)
    send_ref[...] = jnp.where(first, bottom, top)


def first_kernel(slots, home, factor, pivots, rows, inv_high, inv_low, keep, send):
    me = lax.axis_index("row")
    core = me % 2

    def one_slot(slot, carry):
        spot = me * slots + slot
        which = jnp.int32(-1)
        for k in range(STEPS):
            which = jnp.where(home[k] == spot, k, which)

        @pl.when(which >= 0)
        def _():
            r0 = pl.multiple_of(slot * BLOCK, BLOCK)
            c0 = pl.multiple_of(which * BLOCK, BLOCK)
            tiles = [
                factor[pl.ds(r0 + h * HALF, HALF), pl.ds(c0 + h * HALF, HALF)]
                for h in range(2)
            ]
            pivot_rows = [pivots[:, pl.ds(c0 + h * HALF, HALF)] for h in range(2)]
            for h, (high, low) in enumerate(invert(tiles, pivot_rows)):
                inv_high[slot, h] = high
                inv_low[slot, h] = low

        return carry

    lax.fori_loop(0, slots, one_slot, 0)
    finish(0, slots, home, factor, rows, inv_high, inv_low, [], keep, send)


def finish(k, slots, home, factor, rows, inv_high, inv_low, solved, keep, send):
    me = lax.axis_index("row")
    core = me % 2
    mine = home[k] // slots == me

    @pl.when(mine)
    def _():
        slot = home[k] % slots
        r0 = pl.multiple_of(slot * BLOCK, BLOCK)
        value = rows[pl.ds(r0, BLOCK), :]
        for j, pair in enumerate(solved):
            for turn, half in enumerate(pair):
                at = core if turn == 0 else 1 - core
                c0 = pl.multiple_of(j * BLOCK + at * HALF, HALF)
                value = value - mm(factor[pl.ds(r0, BLOCK), pl.ds(c0, HALF)], half[...])
        cross = factor[pl.ds(r0 + HALF, HALF), pl.ds(k * BLOCK, HALF)]
        inv = [(inv_high[slot, h], inv_low[slot, h]) for h in range(2)]
        top, bottom = solve(cross, inv, value)
        put_halves(core, top, bottom, keep, send)

    @pl.when(jnp.logical_not(mine))
    def _():
        keep[...] = jnp.zeros_like(keep)
        send[...] = jnp.zeros_like(send)


def step_kernel(k, slots, home, factor, rows, inv_high, inv_low, *refs):
    solved = [(refs[2 * j], refs[2 * j + 1]) for j in range(k)]
    keep, send = refs[2 * k :]
    finish(k, slots, home, factor, rows, inv_high, inv_low, solved, keep, send)


def last_kernel(slots, home, factor, rows, *refs):
    me = lax.axis_index("row")
    core = me % 2
    solved = [(refs[2 * j], refs[2 * j + 1]) for j in range(STEPS)]
    out = refs[2 * STEPS]
    eye_shape = (HALF, HALF)
    eye = (
        lax.broadcasted_iota(jnp.int32, eye_shape, 0)
        == lax.broadcasted_iota(jnp.int32, eye_shape, 1)
    ).astype(F32).astype(BF)
    columns = rows.shape[1]

    def chunk(at, carry):
        r0 = pl.multiple_of(at * HALF, HALF)
        value = rows[pl.ds(r0, HALF), :]
        for j, pair in enumerate(solved):
            for turn, half in enumerate(pair):
                where = core if turn == 0 else 1 - core
                c0 = pl.multiple_of(j * BLOCK + where * HALF, HALF)
                value = value - mm(factor[pl.ds(r0, HALF), pl.ds(c0, HALF)], half[...])
        value = value.astype(BF)
        for c in range(0, columns, HALF):
            out[c : c + HALF, pl.ds(r0, HALF)] = mm_nt(eye, value[:, c : c + HALF]).astype(BF)
        return carry

    lax.fori_loop(0, rows.shape[0] // HALF, chunk, 0)


def order_kernel(slots, width, home, arrived, *refs):
    me = lax.axis_index("row")
    core = me % 2
    solved = [(refs[2 * j], refs[2 * j + 1]) for j in range(STEPS)]
    out, variance = refs[2 * STEPS :]
    columns = solved[0][0].shape[1]
    pick = (
        lax.broadcasted_iota(jnp.int32, (width, columns), 1)
        == lax.broadcasted_iota(jnp.int32, (width, columns), 0) + me * width
    ).astype(F32).astype(BF)
    total = jnp.zeros((width, 1), F32)
    for j, pair in enumerate(solved):
        for turn, half in enumerate(pair):
            where = core if turn == 0 else 1 - core
            c0 = pl.multiple_of(j * BLOCK + where * HALF, HALF)
            value = mm_nt(pick, half[...])
            out[:, pl.ds(c0, HALF)] = value
            total = total + jnp.sum(value * value, axis=1, keepdims=True)
    variance[...] = jnp.broadcast_to(total * (1.0 / (STEPS * BLOCK)), variance.shape)
    blocks = out.shape[1] // BLOCK

    def place(g, carry):
        spot = home[g]
        r0 = pl.multiple_of((spot // slots) * width, width)
        c0 = pl.multiple_of((spot % slots) * BLOCK, BLOCK)
        o0 = pl.multiple_of(g * BLOCK, BLOCK)
        out[:, pl.ds(o0, BLOCK)] = arrived[pl.ds(r0, width), pl.ds(c0, BLOCK)].astype(F32)
        return carry

    lax.fori_loop(STEPS, blocks, place, 0)


def call(kernel, count, outs, flops=0, moved=0):
    vmem = pl.BlockSpec(memory_space=pltpu.VMEM)
    return pl.pallas_call(
        kernel,
        grid_spec=pltpu.PrefetchScalarGridSpec(
            num_scalar_prefetch=1,
            in_specs=[vmem] * count,
            out_specs=[vmem] * len(outs),
        ),
        out_shape=outs,
        compiler_params=pltpu.CompilerParams(vmem_limit_bytes=VMEM_LIMIT),
        cost_estimate=pl.CostEstimate(flops=flops, bytes_accessed=moved, transcendentals=0),
    )


def hop(value, count, mask):
    return lax.ppermute(value, "row", [(i, i ^ mask) for i in range(count)])


def spread(keep, send, count):
    mine = keep + hop(send, count, 1)
    if count >= 8:
        mine = mine + hop(mine, count, 2) + hop(mine, count, 4) + hop(mine, count, 6)
        mask = 8
    else:
        mask = 2
    while mask < count:
        mine = mine + hop(mine, count, mask)
        mask *= 2
    return mine, hop(mine, count, 1)


def on_device(factor_panel, pivots, right_sides, block_home):
    slots = factor_panel.shape[0] // BLOCK
    columns = right_sides.shape[1]
    count = lax.axis_size("row")
    width = columns // count
    blocks = block_home.shape[0]
    half = jax.ShapeDtypeStruct((HALF, columns), BF)
    inverse = jax.ShapeDtypeStruct((slots, 2, HALF, HALF), BF)
    inv_high, inv_low, keep, send = call(
        functools.partial(first_kernel, slots), 3, [inverse, inverse, half, half]
    )(block_home, factor_panel, pivots.reshape(1, PANEL), right_sides)
    solved = list(spread(keep, send, count))
    for k in range(1, STEPS):
        keep, send = call(functools.partial(step_kernel, k, slots), 4 + 2 * k, [half, half])(
            block_home, factor_panel, right_sides, inv_high, inv_low, *solved
        )
        solved += spread(keep, send, count)
    (turned,) = call(
        functools.partial(last_kernel, slots),
        2 + 2 * STEPS,
        [jax.ShapeDtypeStruct((columns, slots * BLOCK), BF)],
    )(block_home, factor_panel, right_sides, *solved)
    arrived = lax.all_to_all(turned, "row", split_axis=0, concat_axis=0, tiled=True)
    out, variance = call(
        functools.partial(order_kernel, slots, width),
        1 + 2 * STEPS,
        [
            jax.ShapeDtypeStruct((width, blocks * BLOCK), F32),
            jax.ShapeDtypeStruct((width, 128), F32),
        ],
    )(block_home, arrived, *solved)
    return out.T, variance[:, 0]


def solution(mesh):
    in_specs = (P(("groups", "row"), None), P("groups"), P(("groups", "row"), None), P())
    out_specs = (P("groups", "row"), P(("groups", "row")))
    return jax.shard_map(
        on_device, mesh=mesh, in_specs=in_specs, out_specs=out_specs, check_vma=False
    )
```

```python
import functools

import jax
import jax.numpy as jnp
from jax import lax
from jax.experimental import pallas as pl
from jax.experimental.pallas import tpu as pltpu
from jax.sharding import PartitionSpec as P

BLOCK = 512
HALF = 256
STEPS = 4
PANEL = 2048
BF = jnp.bfloat16
F32 = jnp.float32
VMEM_LIMIT = 24 * 1024 * 1024


def mm(a, b):
    return jnp.dot(a, b, preferred_element_type=F32)


def mm_nt(a, b):
    return lax.dot_general(a, b, (((1,), (1,)), ((), ())), preferred_element_type=F32)


def parts(value):
    high = value.astype(BF)
    return high, (value - high.astype(F32)).astype(BF)


def mm3(a_high, a_low, b):
    b_high, b_low = parts(b)
    return mm(a_high, b_high) + (mm(a_high, b_low) + mm(a_low, b_high))


def odd_rows(value, size):
    picked = [value[at : at + size] for at in range(size, value.shape[0], 2 * size)]
    return picked[0] if len(picked) == 1 else jnp.concatenate(picked, axis=0)


def put_odd_rows(value, odd, size):
    pieces = []
    for at in range(0, value.shape[0], size):
        turn = at // size
        pieces.append(
            value[at : at + size] if turn % 2 == 0 else odd[turn // 2 * size : (turn // 2 + 1) * size]
        )
    return jnp.concatenate(pieces, axis=0)


def double(tile, inverse, halves, size, apart, lower):
    high, low = halves
    width = tile.shape[1]
    link = jnp.where((lax.shift_right_logical(apart, size.bit_length() - 1) == 1) & lower, tile, 0.0)
    link = link.astype(BF)
    packed = size >= 16
    if packed:
        link = odd_rows(link, size)
        left_high, left_low = odd_rows(high, size), odd_rows(low, size)
    else:
        left_high, left_low = high, low
    if width <= 128:
        both = mm(link, jnp.concatenate([high, low], axis=1))
        inner = both[:, :width] + both[:, width:]
    else:
        inner = mm(link, high) + mm(link, low)
    if packed:
        zero = jnp.zeros((size, width), F32)
        pieces = []
        for at in range(inner.shape[0] // size):
            pieces += [zero, inner[at * size : (at + 1) * size]]
        inner = jnp.concatenate(pieces, axis=0)
    inner_high, inner_low = parts(inner)
    if width <= 128:
        rows = left_high.shape[0]
        both = mm(
            jnp.concatenate([left_high, left_low], axis=0),
            jnp.concatenate([inner_high, inner_low], axis=1),
        )
        change = both[:rows, :width] + (both[:rows, width:] + both[rows:, :width])
    else:
        change = mm(left_high, inner_high) + (mm(left_high, inner_low) + mm(left_low, inner_high))
    if packed:
        inverse = put_odd_rows(inverse, odd_rows(inverse, size) - change, size)
    else:
        inverse = inverse - change
    return inverse, parts(inverse)


def index_maps(shape):
    row = lax.broadcasted_iota(jnp.int32, shape, 0)
    col = lax.broadcasted_iota(jnp.int32, shape, 1)
    return row == col, row ^ col, row > col


def invert(tiles, pivot_rows):
    quarter = HALF // 2
    on, apart, lower = index_maps((quarter, quarter))
    small, values = [], []
    for tile, pivot in zip(tiles, pivot_rows):
        for at in range(0, HALF, quarter):
            piece = tile[at : at + quarter, at : at + quarter].astype(F32)
            across = 1.0 / pivot[:, at : at + quarter]
            diag = jnp.where(on, across, 0.0)
            down = jnp.sum(diag, axis=1, keepdims=True)
            first = jnp.where((apart == 1) & lower, piece, 0.0)
            small.append(piece)
            values.append(diag - down * first * across)
    halves = [parts(value) for value in values]
    size = 2
    while size < quarter:
        for at, piece in enumerate(small):
            values[at], halves[at] = double(piece, values[at], halves[at], size, apart, lower)
        size *= 2
    zero = jnp.zeros((quarter, quarter), F32)
    _, apart, lower = index_maps((HALF, HALF))
    result = []
    for at, tile in enumerate(tiles):
        value = jnp.concatenate(
            [
                jnp.concatenate([values[2 * at], zero], axis=1),
                jnp.concatenate([zero, values[2 * at + 1]], axis=1),
            ],
            axis=0,
        )
        result.append(double(tile.astype(F32), value, parts(value), quarter, apart, lower)[1])
    return result


def solve(tile_cross, inv, rows):
    (a_high, a_low), (b_high, b_low) = inv
    top = mm3(a_high, a_low, rows[:HALF])
    top_high, top_low = parts(top)
    rest = rows[HALF:] - (mm(tile_cross, top_high) + mm(tile_cross, top_low))
    return top.astype(BF), mm3(b_high, b_low, rest).astype(BF)


def put_halves(core, top, bottom, keep_ref, send_ref):
    first = core == 0
    keep_ref[...] = jnp.where(first, top, bottom)
    send_ref[...] = jnp.where(first, bottom, top)


def first_kernel(slots, home_ref, factor, pivots, rows, inv_high, inv_low, keep, send,
                 home, tiles, pivot, value, sems):
    me = lax.axis_index("row")
    fetch_home = pltpu.make_async_copy(home_ref, home, sems.at[0])
    fetch_pivot = pltpu.make_async_copy(pivots, pivot, sems.at[1])
    fetch_home.start()
    fetch_pivot.start()
    fetch_home.wait()
    which = []
    for slot in range(slots):
        found = jnp.int32(-1)
        for k in range(STEPS):
            found = jnp.where(home[k] == me * slots + slot, k, found)
        which.append(found)
    mine = home[0] // slots == me
    first_slot = home[0] % slots
    fetch_rows = pltpu.make_async_copy(
        rows.at[pl.ds(pl.multiple_of(first_slot * BLOCK, BLOCK), BLOCK), :], value, sems.at[2]
    )

    def fetch_tile(slot):
        c0 = pl.multiple_of(jnp.maximum(which[slot], 0) * BLOCK, BLOCK)
        return pltpu.make_async_copy(
            factor.at[pl.ds(slot * BLOCK, BLOCK), pl.ds(c0, BLOCK)],
            tiles.at[pl.ds(slot * BLOCK, BLOCK), :],
            sems.at[3 + slot],
        )

    for slot in range(slots):

        @pl.when(which[slot] >= 0)
        def _(slot=slot):
            fetch_tile(slot).start()

    @pl.when(mine)
    def _():
        fetch_rows.start()

    fetch_pivot.wait()
    for slot in range(slots):

        @pl.when(which[slot] >= 0)
        def _(slot=slot):
            fetch_tile(slot).wait()

    def one_slot(slot, carry):
        at = which[0]
        for other in range(1, slots):
            at = jnp.where(slot == other, which[other], at)

        @pl.when(at >= 0)
        def _():
            r0 = pl.multiple_of(slot * BLOCK, BLOCK)
            c0 = pl.multiple_of(at * BLOCK, BLOCK)
            pieces = [
                tiles[pl.ds(r0 + h * HALF, HALF), h * HALF : (h + 1) * HALF] for h in range(2)
            ]
            pivot_rows = [pivot[:, pl.ds(c0 + h * HALF, HALF)] for h in range(2)]
            for h, (high, low) in enumerate(invert(pieces, pivot_rows)):
                inv_high[slot, h] = high
                inv_low[slot, h] = low

        return carry

    lax.fori_loop(0, slots, one_slot, 0)

    @pl.when(mine)
    def _():
        fetch_rows.wait()
        r0 = pl.multiple_of(first_slot * BLOCK + HALF, HALF)
        inv = [(inv_high[first_slot, h], inv_low[first_slot, h]) for h in range(2)]
        top, bottom = solve(tiles[pl.ds(r0, HALF), :HALF], inv, value[...])
        put_halves(me % 2, top, bottom, keep, send)

    @pl.when(jnp.logical_not(mine))
    def _():
        keep[...] = jnp.zeros_like(keep)
        send[...] = jnp.zeros_like(send)


def finish(k, slots, home, factor, rows, inv_high, inv_low, solved, keep, send):
    me = lax.axis_index("row")
    core = me % 2
    mine = home[k] // slots == me

    @pl.when(mine)
    def _():
        slot = home[k] % slots
        r0 = pl.multiple_of(slot * BLOCK, BLOCK)
        value = rows[pl.ds(r0, BLOCK), :]
        for j, pair in enumerate(solved):
            for turn, half in enumerate(pair):
                at = core if turn == 0 else 1 - core
                c0 = pl.multiple_of(j * BLOCK + at * HALF, HALF)
                value = value - mm(factor[pl.ds(r0, BLOCK), pl.ds(c0, HALF)], half[...])
        cross = factor[pl.ds(r0 + HALF, HALF), pl.ds(k * BLOCK, HALF)]
        inv = [(inv_high[slot, h], inv_low[slot, h]) for h in range(2)]
        top, bottom = solve(cross, inv, value)
        put_halves(core, top, bottom, keep, send)

    @pl.when(jnp.logical_not(mine))
    def _():
        keep[...] = jnp.zeros_like(keep)
        send[...] = jnp.zeros_like(send)


def step_kernel(k, slots, home, factor, rows, inv_high, inv_low, *refs):
    solved = [(refs[2 * j], refs[2 * j + 1]) for j in range(k)]
    keep, send = refs[2 * k :]
    finish(k, slots, home, factor, rows, inv_high, inv_low, solved, keep, send)


def turn(core, at, number):
    where = core if number == 0 else 1 - core
    return pl.multiple_of(at * BLOCK + where * HALF, HALF)


def columns_of(half, me, width):
    columns = half.shape[1]
    pick = (
        lax.broadcasted_iota(jnp.int32, (width, columns), 1)
        == lax.broadcasted_iota(jnp.int32, (width, columns), 0) + me * width
    ).astype(F32).astype(BF)
    return mm_nt(pick, half)


def row_of_squares(value):
    high, low = parts(value * value)
    ones = jnp.ones((8, value.shape[1]), BF)
    return (mm_nt(ones, high) + mm_nt(ones, low))[:1]


def early_kernel(width, factor, rows, after, *refs):
    me = lax.axis_index("row")
    core = me % 2
    count = STEPS - 1
    solved = [(refs[2 * j], refs[2 * j + 1]) for j in range(count)]
    rest, own, squares = refs[2 * count :]

    def chunk(at, carry):
        r0 = pl.multiple_of(at * HALF, HALF)
        value = rows[pl.ds(r0, HALF), :]
        for j, pair in enumerate(solved):
            for number, half in enumerate(pair):
                c0 = turn(core, j, number)
                value = value - mm(factor[pl.ds(r0, HALF), pl.ds(c0, HALF)], half[...])
        rest[pl.ds(r0, HALF), :] = value
        return carry

    lax.fori_loop(0, rows.shape[0] // HALF, chunk, 0)
    total = jnp.zeros((1, width), F32)
    for j, pair in enumerate(solved):
        for number, half in enumerate(pair):
            value = columns_of(half[...], me, width)
            own[:, pl.ds(turn(core, j, number), HALF)] = value
            total = total + row_of_squares(value)
    squares[...] = total


def last_kernel(factor, rest, *refs):
    core = lax.axis_index("row") % 2
    pair, out = refs[:2], refs[2]
    on, _, _ = index_maps((HALF, HALF))
    eye = on.astype(F32).astype(BF)
    columns = rest.shape[1]

    def chunk(at, carry):
        r0 = pl.multiple_of(at * HALF, HALF)
        value = rest[pl.ds(r0, HALF), :]
        for number, half in enumerate(pair):
            c0 = turn(core, STEPS - 1, number)
            value = value - mm(factor[pl.ds(r0, HALF), pl.ds(c0, HALF)], half[...])
        value = value.astype(BF)
        for c in range(0, columns, HALF):
            out[c : c + HALF, pl.ds(r0, HALF)] = mm_nt(eye, value[:, c : c + HALF]).astype(BF)
        return carry

    lax.fori_loop(0, rest.shape[0] // HALF, chunk, 0)


def order_kernel(slots, width, home, arrived, own, squares, mine, other, out, variance, held, sems):
    me = lax.axis_index("row")
    core = me % 2
    solved_rows = (STEPS - 1) * BLOCK
    blocks = held.shape[1] // BLOCK
    group = 4

    def put_out(at):
        span = pl.ds(pl.multiple_of(at * group * BLOCK, BLOCK), group * BLOCK)
        return pltpu.make_async_copy(held.at[:, span], out.at[:, span], sems.at[at])

    def place_group(at, carry):
        for turn_at in range(group):
            g = at * group + turn_at
            spot = home[g]
            r0 = pl.multiple_of((spot // slots) * width, width)
            c0 = pl.multiple_of((spot % slots) * BLOCK, BLOCK)
            o0 = pl.multiple_of(g * BLOCK, BLOCK)
            held[:, pl.ds(o0, BLOCK)] = arrived[pl.ds(r0, width), pl.ds(c0, BLOCK)].astype(F32)
        put_out(at).start()
        return carry

    held[:, :solved_rows] = own[...]
    total = squares[...]
    for number, half in enumerate((mine, other)):
        value = columns_of(half[...], me, width)
        held[:, pl.ds(turn(core, STEPS - 1, number), HALF)] = value
        total = total + row_of_squares(value)
    variance[...] = total * (1.0 / (STEPS * BLOCK))
    put_out(0).start()
    lax.fori_loop(1, blocks // group, place_group, 0)

    def drain(at, carry):
        put_out(at).wait()
        return carry

    lax.fori_loop(0, blocks // group, drain, 0)


def call(kernel, outs, in_specs, out_specs, scalars=0, scratch=(), flops=0):
    return pl.pallas_call(
        kernel,
        grid_spec=pltpu.PrefetchScalarGridSpec(
            num_scalar_prefetch=scalars,
            in_specs=in_specs,
            out_specs=out_specs,
            scratch_shapes=scratch,
        ),
        out_shape=outs,
        compiler_params=pltpu.CompilerParams(vmem_limit_bytes=VMEM_LIMIT),
        cost_estimate=pl.CostEstimate(flops=flops, bytes_accessed=0, transcendentals=0),
    )


def hop(value, count, mask):
    return lax.ppermute(value, "row", [(i, i ^ mask) for i in range(count)])


def spread(keep, send, count, beside=()):
    mine = keep + hop(send, count, 1)
    if count >= 8:
        mine = mine + hop(mine, count, 2) + hop(mine, count, 4) + hop(mine, count, 6)
        mask = 8
        if beside:
            mine, *beside = lax.optimization_barrier((mine, *beside))
    else:
        mask = 2
    while mask < count:
        mine = mine + hop(mine, count, mask)
        mask *= 2
    return [mine, hop(mine, count, 1), *beside]


def on_device(factor_panel, pivots, right_sides, block_home):
    slots = factor_panel.shape[0] // BLOCK
    held_rows, columns = right_sides.shape
    count = lax.axis_size("row")
    width = columns // count
    blocks = block_home.shape[0]
    total = blocks * BLOCK
    shape = jax.ShapeDtypeStruct
    half = shape((HALF, columns), BF)
    inverse = shape((slots, 2, HALF, HALF), BF)
    vmem = pl.BlockSpec(memory_space=pltpu.VMEM)
    hbm = pl.BlockSpec(memory_space=pltpu.HBM)
    inv_high, inv_low, keep, send = call(
        functools.partial(first_kernel, slots),
        [inverse, inverse, half, half],
        [hbm] * 4,
        [vmem] * 4,
        scratch=(
            pltpu.SMEM((blocks,), jnp.int32),
            pltpu.VMEM((slots * BLOCK, BLOCK), BF),
            pltpu.VMEM((1, PANEL), F32),
            pltpu.VMEM((BLOCK, columns), F32),
            pltpu.SemaphoreType.DMA((3 + slots,)),
        ),
    )(*(
        pltpu.with_memory_space_constraint(value, pltpu.HBM)
        for value in (block_home, factor_panel, pivots.reshape(1, PANEL), right_sides)
    ))
    solved = spread(keep, send, count)
    for k in range(1, STEPS):
        keep, send = call(
            functools.partial(step_kernel, k, slots),
            [half, half],
            [vmem] * (4 + 2 * k),
            [vmem] * 2,
            scalars=1,
        )(block_home, factor_panel, right_sides, inv_high, inv_low, *solved)
        beside = ()
        if k == STEPS - 1:
            beside = call(
                functools.partial(early_kernel, width),
                [shape((held_rows, columns), F32), shape((width, k * BLOCK), F32), shape((1, width), F32)],
                [vmem] * (3 + 2 * k),
                [vmem] * 3,
                flops=2 * held_rows * columns * k * BLOCK,
            )(factor_panel, right_sides, send, *solved)
        solved += spread(keep, send, count, beside)
    *solved, rest, own, squares = solved
    (turned,) = call(
        last_kernel, [shape((columns, held_rows), BF)], [vmem] * 4, [vmem]
    )(factor_panel, rest, *solved[-2:])
    arrived = lax.all_to_all(turned, "row", split_axis=0, concat_axis=0, tiled=True)
    out, variance = call(
        functools.partial(order_kernel, slots, width),
        [shape((width, total), F32), shape((1, width), F32)],
        [vmem] * 5,
        [hbm, vmem],
        scalars=1,
        scratch=(pltpu.VMEM((width, total), F32), pltpu.SemaphoreType.DMA((blocks // 4,))),
    )(block_home, arrived, own, squares, *solved[-2:])
    return out.T, variance[0]


def solution(mesh):
    in_specs = (P(("groups", "row"), None), P("groups"), P(("groups", "row"), None), P())
    out_specs = (P("groups", "row"), P(("groups", "row")))
    return jax.shard_map(
        on_device, mesh=mesh, in_specs=in_specs, out_specs=out_specs, check_vma=False
    )
```

```python
import functools

import jax
import jax.numpy as jnp
from jax import lax
from jax.experimental import pallas as pl
from jax.experimental.pallas import tpu as pltpu
from jax.sharding import PartitionSpec as P

BLOCK = 512
HALF = 256
STEPS = 4
PANEL = 2048
BF = jnp.bfloat16
F32 = jnp.float32
VMEM_LIMIT = 24 * 1024 * 1024


def mm(a, b):
    return jnp.dot(a, b, preferred_element_type=F32)


def mm_nt(a, b):
    return lax.dot_general(a, b, (((1,), (1,)), ((), ())), preferred_element_type=F32)


def parts(value):
    high = value.astype(BF)
    return high, (value - high.astype(F32)).astype(BF)


def mm3(a_high, a_low, b):
    b_high, b_low = parts(b)
    return mm(a_high, b_high) + (mm(a_high, b_low) + mm(a_low, b_high))


def odd_rows(value, size):
    picked = [value[at : at + size] for at in range(size, value.shape[0], 2 * size)]
    return picked[0] if len(picked) == 1 else jnp.concatenate(picked, axis=0)


def put_odd_rows(value, odd, size):
    pieces = []
    for at in range(0, value.shape[0], size):
        turn = at // size
        pieces.append(
            value[at : at + size] if turn % 2 == 0 else odd[turn // 2 * size : (turn // 2 + 1) * size]
        )
    return jnp.concatenate(pieces, axis=0)


def double(tile, inverse, halves, size, apart, lower):
    high, low = halves
    width = tile.shape[1]
    link = jnp.where((lax.shift_right_logical(apart, size.bit_length() - 1) == 1) & lower, tile, 0.0)
    link = link.astype(BF)
    packed = size >= 16
    if packed:
        link = odd_rows(link, size)
        left_high, left_low = odd_rows(high, size), odd_rows(low, size)
    else:
        left_high, left_low = high, low
    if width <= 128:
        both = mm(link, jnp.concatenate([high, low], axis=1))
        inner = both[:, :width] + both[:, width:]
    else:
        inner = mm(link, high) + mm(link, low)
    if packed:
        zero = jnp.zeros((size, width), F32)
        pieces = []
        for at in range(inner.shape[0] // size):
            pieces += [zero, inner[at * size : (at + 1) * size]]
        inner = jnp.concatenate(pieces, axis=0)
    inner_high, inner_low = parts(inner)
    if width <= 128:
        rows = left_high.shape[0]
        both = mm(
            jnp.concatenate([left_high, left_low], axis=0),
            jnp.concatenate([inner_high, inner_low], axis=1),
        )
        change = both[:rows, :width] + (both[:rows, width:] + both[rows:, :width])
    else:
        change = mm(left_high, inner_high) + (mm(left_high, inner_low) + mm(left_low, inner_high))
    if packed:
        inverse = put_odd_rows(inverse, odd_rows(inverse, size) - change, size)
    else:
        inverse = inverse - change
    return inverse, parts(inverse)


def index_maps(shape):
    row = lax.broadcasted_iota(jnp.int32, shape, 0)
    col = lax.broadcasted_iota(jnp.int32, shape, 1)
    return row == col, row ^ col, row > col


def invert(tiles, pivot_rows):
    quarter = HALF // 2
    on, apart, lower = index_maps((quarter, quarter))
    small, values = [], []
    for tile, pivot in zip(tiles, pivot_rows):
        for at in range(0, HALF, quarter):
            piece = tile[at : at + quarter, at : at + quarter].astype(F32)
            across = 1.0 / pivot[:, at : at + quarter]
            diag = jnp.where(on, across, 0.0)
            down = jnp.sum(diag, axis=1, keepdims=True)
            first = jnp.where((apart == 1) & lower, piece, 0.0)
            small.append(piece)
            values.append(diag - down * first * across)
    halves = [parts(value) for value in values]
    size = 2
    while size < quarter:
        for at, piece in enumerate(small):
            values[at], halves[at] = double(piece, values[at], halves[at], size, apart, lower)
        size *= 2
    zero = jnp.zeros((quarter, quarter), F32)
    _, apart, lower = index_maps((HALF, HALF))
    result = []
    for at, tile in enumerate(tiles):
        value = jnp.concatenate(
            [
                jnp.concatenate([values[2 * at], zero], axis=1),
                jnp.concatenate([zero, values[2 * at + 1]], axis=1),
            ],
            axis=0,
        )
        result.append(double(tile.astype(F32), value, parts(value), quarter, apart, lower)[1])
    return result


def solve(tile_cross, inv, rows):
    (a_high, a_low), (b_high, b_low) = inv
    top = mm3(a_high, a_low, rows[:HALF])
    top_high, top_low = parts(top)
    rest = rows[HALF:] - (mm(tile_cross, top_high) + mm(tile_cross, top_low))
    return top.astype(BF), mm3(b_high, b_low, rest).astype(BF)


def put_halves(core, top, bottom, keep_ref, send_ref):
    first = core == 0
    keep_ref[...] = jnp.where(first, top, bottom)
    send_ref[...] = jnp.where(first, bottom, top)


def first_kernel(slots, home_ref, factor, pivots, rows, inv_high, inv_low, keep, send,
                 home, tiles, pivot, value, sems):
    me = lax.axis_index("row")
    fetch_home = pltpu.make_async_copy(home_ref, home, sems.at[0])
    fetch_pivot = pltpu.make_async_copy(pivots, pivot, sems.at[1])
    fetch_home.start()
    fetch_pivot.start()
    fetch_home.wait()
    which = []
    for slot in range(slots):
        found = jnp.int32(-1)
        for k in range(STEPS):
            found = jnp.where(home[k] == me * slots + slot, k, found)
        which.append(found)
    mine = home[0] // slots == me
    first_slot = home[0] % slots
    fetch_rows = pltpu.make_async_copy(
        rows.at[pl.ds(pl.multiple_of(first_slot * BLOCK, BLOCK), BLOCK), :], value, sems.at[2]
    )

    def fetch_tile(slot):
        c0 = pl.multiple_of(jnp.maximum(which[slot], 0) * BLOCK, BLOCK)
        return pltpu.make_async_copy(
            factor.at[pl.ds(slot * BLOCK, BLOCK), pl.ds(c0, BLOCK)],
            tiles.at[pl.ds(slot * BLOCK, BLOCK), :],
            sems.at[3 + slot],
        )

    for slot in range(slots):

        @pl.when(which[slot] >= 0)
        def _(slot=slot):
            fetch_tile(slot).start()

    @pl.when(mine)
    def _():
        fetch_rows.start()

    fetch_pivot.wait()
    for slot in range(slots):

        @pl.when(which[slot] >= 0)
        def _(slot=slot):
            fetch_tile(slot).wait()

    def one_slot(slot, carry):
        at = which[0]
        for other in range(1, slots):
            at = jnp.where(slot == other, which[other], at)

        @pl.when(at >= 0)
        def _():
            r0 = pl.multiple_of(slot * BLOCK, BLOCK)
            c0 = pl.multiple_of(at * BLOCK, BLOCK)
            pieces = [
                tiles[pl.ds(r0 + h * HALF, HALF), h * HALF : (h + 1) * HALF] for h in range(2)
            ]
            pivot_rows = [pivot[:, pl.ds(c0 + h * HALF, HALF)] for h in range(2)]
            for h, (high, low) in enumerate(invert(pieces, pivot_rows)):
                inv_high[slot, h] = high
                inv_low[slot, h] = low

        return carry

    lax.fori_loop(0, slots, one_slot, 0)

    @pl.when(mine)
    def _():
        fetch_rows.wait()
        r0 = pl.multiple_of(first_slot * BLOCK + HALF, HALF)
        inv = [(inv_high[first_slot, h], inv_low[first_slot, h]) for h in range(2)]
        top, bottom = solve(tiles[pl.ds(r0, HALF), :HALF], inv, value[...])
        put_halves(me % 2, top, bottom, keep, send)

    @pl.when(jnp.logical_not(mine))
    def _():
        keep[...] = jnp.zeros_like(keep)
        send[...] = jnp.zeros_like(send)


def step_kernel(k, slots, home, factor, rest, inv_high, inv_low, mine, other, keep, send):
    me = lax.axis_index("row")
    core = me % 2
    owner = home[k] // slots == me

    @pl.when(owner)
    def _():
        slot = home[k] % slots
        r0 = pl.multiple_of(slot * BLOCK, BLOCK)
        value = rest[pl.ds(r0, BLOCK), :]
        for number, half in enumerate((mine, other)):
            c0 = turn(core, k - 1, number)
            value = value - mm(factor[pl.ds(r0, BLOCK), pl.ds(c0, HALF)], half[...])
        cross = factor[pl.ds(r0 + HALF, HALF), pl.ds(k * BLOCK, HALF)]
        inv = [(inv_high[slot, h], inv_low[slot, h]) for h in range(2)]
        top, bottom = solve(cross, inv, value)
        put_halves(core, top, bottom, keep, send)

    @pl.when(jnp.logical_not(owner))
    def _():
        keep[...] = jnp.zeros_like(keep)
        send[...] = jnp.zeros_like(send)


def turn(core, at, number):
    where = core if number == 0 else 1 - core
    return pl.multiple_of(at * BLOCK + where * HALF, HALF)


def columns_of(half, me, width):
    columns = half.shape[1]
    pick = (
        lax.broadcasted_iota(jnp.int32, (width, columns), 1)
        == lax.broadcasted_iota(jnp.int32, (width, columns), 0) + me * width
    ).astype(F32).astype(BF)
    return mm_nt(pick, half)


def row_of_squares(value):
    high, low = parts(value * value)
    ones = jnp.ones((8, value.shape[1]), BF)
    return (mm_nt(ones, high) + mm_nt(ones, low))[:1]


def early_kernel(k, width, factor, before, after, mine, other, rest, own, squares):
    me = lax.axis_index("row")
    core = me % 2

    def chunk(at, carry):
        r0 = pl.multiple_of(at * HALF, HALF)
        value = before[pl.ds(r0, HALF), :]
        for number, half in enumerate((mine, other)):
            c0 = turn(core, k, number)
            value = value - mm(factor[pl.ds(r0, HALF), pl.ds(c0, HALF)], half[...])
        rest[pl.ds(r0, HALF), :] = value
        return carry

    lax.fori_loop(0, before.shape[0] // HALF, chunk, 0)
    own_columns(core, me, width, mine, other, own, squares)


def own_columns(core, me, width, mine, other, own, squares):
    total = jnp.zeros((1, width), F32)
    for number, half in enumerate((mine, other)):
        value = columns_of(half[...], me, width)
        own[:, pl.ds(turn(core, 0, number), HALF)] = value
        total = total + row_of_squares(value)
    squares[...] = total


def last_kernel(factor, rest, *refs):
    core = lax.axis_index("row") % 2
    pair, out = refs[:2], refs[2]
    on, _, _ = index_maps((HALF, HALF))
    eye = on.astype(F32).astype(BF)
    columns = rest.shape[1]

    def chunk(at, carry):
        r0 = pl.multiple_of(at * HALF, HALF)
        value = rest[pl.ds(r0, HALF), :]
        for number, half in enumerate(pair):
            c0 = turn(core, STEPS - 1, number)
            value = value - mm(factor[pl.ds(r0, HALF), pl.ds(c0, HALF)], half[...])
        value = value.astype(BF)
        for c in range(0, columns, HALF):
            out[c : c + HALF, pl.ds(r0, HALF)] = mm_nt(eye, value[:, c : c + HALF]).astype(BF)
        return carry

    lax.fori_loop(0, rest.shape[0] // HALF, chunk, 0)


def order_kernel(slots, width, home, arrived, mine, other, *refs):
    owns, squares = refs[: STEPS - 1], refs[STEPS - 1 : 2 * (STEPS - 1)]
    out, variance, held, sems = refs[2 * (STEPS - 1) :]
    me = lax.axis_index("row")
    core = me % 2
    blocks = held.shape[1] // BLOCK
    group = STEPS

    def put_out(at):
        span = pl.ds(pl.multiple_of(at * group * BLOCK, BLOCK), group * BLOCK)
        return pltpu.make_async_copy(held.at[:, span], out.at[:, span], sems.at[at])

    def place_group(at, carry):
        for turn_at in range(group):
            g = at * group + turn_at
            spot = home[g]
            r0 = pl.multiple_of((spot // slots) * width, width)
            c0 = pl.multiple_of((spot % slots) * BLOCK, BLOCK)
            o0 = pl.multiple_of(g * BLOCK, BLOCK)
            held[:, pl.ds(o0, BLOCK)] = arrived[pl.ds(r0, width), pl.ds(c0, BLOCK)].astype(F32)
        put_out(at).start()
        return carry

    total = jnp.zeros((1, width), F32)
    for j in range(STEPS - 1):
        held[:, j * BLOCK : (j + 1) * BLOCK] = owns[j][...]
        total = total + squares[j][...]
    for number, half in enumerate((mine, other)):
        value = columns_of(half[...], me, width)
        held[:, pl.ds(turn(core, STEPS - 1, number), HALF)] = value
        total = total + row_of_squares(value)
    variance[...] = total * (1.0 / (STEPS * BLOCK))
    put_out(0).start()
    lax.fori_loop(1, blocks // group, place_group, 0)

    def drain(at, carry):
        put_out(at).wait()
        return carry

    lax.fori_loop(0, blocks // group, drain, 0)


def call(kernel, outs, in_specs, out_specs, scalars=0, scratch=(), flops=0):
    return pl.pallas_call(
        kernel,
        grid_spec=pltpu.PrefetchScalarGridSpec(
            num_scalar_prefetch=scalars,
            in_specs=in_specs,
            out_specs=out_specs,
            scratch_shapes=scratch,
        ),
        out_shape=outs,
        compiler_params=pltpu.CompilerParams(vmem_limit_bytes=VMEM_LIMIT),
        cost_estimate=pl.CostEstimate(flops=flops, bytes_accessed=0, transcendentals=0),
    )


def hop(value, count, even, odd):
    return lax.ppermute(
        value, "row", [(i, i ^ (odd if i % 2 else even)) for i in range(count)]
    )


def spread(keep, send, count, beside=()):
    mine = keep + hop(send, count, 1, 1)
    masks = [1 << bit for bit in range(1, count.bit_length() - 1)]
    for at, mask in enumerate(masks):
        mine = mine + hop(mine, count, mask, masks[at - 1])
        if beside and at == 0:
            mine, *beside = lax.optimization_barrier((mine, *beside))
    return [mine, hop(mine, count, 1, 1)], beside


def on_device(factor_panel, pivots, right_sides, block_home):
    slots = factor_panel.shape[0] // BLOCK
    held_rows, columns = right_sides.shape
    count = lax.axis_size("row")
    width = columns // count
    blocks = block_home.shape[0]
    total = blocks * BLOCK
    shape = jax.ShapeDtypeStruct
    half = shape((HALF, columns), BF)
    inverse = shape((slots, 2, HALF, HALF), BF)
    vmem = pl.BlockSpec(memory_space=pltpu.VMEM)
    hbm = pl.BlockSpec(memory_space=pltpu.HBM)
    inv_high, inv_low, keep, send = call(
        functools.partial(first_kernel, slots),
        [inverse, inverse, half, half],
        [hbm] * 4,
        [vmem] * 4,
        scratch=(
            pltpu.SMEM((blocks,), jnp.int32),
            pltpu.VMEM((slots * BLOCK, BLOCK), BF),
            pltpu.VMEM((1, PANEL), F32),
            pltpu.VMEM((BLOCK, columns), F32),
            pltpu.SemaphoreType.DMA((3 + slots,)),
        ),
    )(*(
        pltpu.with_memory_space_constraint(value, pltpu.HBM)
        for value in (block_home, factor_panel, pivots.reshape(1, PANEL), right_sides)
    ))
    (mine, other), _ = spread(keep, send, count)
    rest = right_sides
    owns, squares = [], []
    for k in range(1, STEPS):
        keep, send = call(
            functools.partial(step_kernel, k, slots),
            [half, half],
            [vmem] * 6,
            [vmem] * 2,
            scalars=1,
        )(block_home, factor_panel, rest, inv_high, inv_low, mine, other)
        beside = call(
            functools.partial(early_kernel, k - 1, width),
            [shape((held_rows, columns), F32), shape((width, BLOCK), F32), shape((1, width), F32)],
            [vmem] * 5,
            [vmem] * 3,
            flops=2 * held_rows * columns * BLOCK,
        )(factor_panel, rest, send, mine, other)
        (mine, other), (rest, own, square) = spread(keep, send, count, beside)
        owns.append(own)
        squares.append(square)
    (turned,) = call(
        last_kernel, [shape((columns, held_rows), BF)], [vmem] * 4, [vmem]
    )(factor_panel, rest, mine, other)
    arrived = lax.all_to_all(turned, "row", split_axis=0, concat_axis=0, tiled=True)
    out, variance = call(
        functools.partial(order_kernel, slots, width),
        [shape((width, total), F32), shape((1, width), F32)],
        [vmem] * (3 + 2 * (STEPS - 1)),
        [hbm, vmem],
        scalars=1,
        scratch=(pltpu.VMEM((width, total), F32), pltpu.SemaphoreType.DMA((blocks // STEPS,))),
    )(block_home, arrived, mine, other, *owns, *squares)
    return out.T, variance[0]


def solution(mesh):
    in_specs = (P(("groups", "row"), None), P("groups"), P(("groups", "row"), None), P())
    out_specs = (P("groups", "row"), P(("groups", "row")))
    return jax.shard_map(
        on_device, mesh=mesh, in_specs=in_specs, out_specs=out_specs, check_vma=False
    )
```

```python
import functools

import jax
import jax.numpy as jnp
from jax import lax
from jax.experimental import pallas as pl
from jax.experimental.pallas import tpu as pltpu
from jax.sharding import PartitionSpec as P

BLOCK = 512
HALF = 256
STEPS = 4
PANEL = 2048
BF = jnp.bfloat16
F32 = jnp.float32
VMEM_LIMIT = 24 * 1024 * 1024


def mm(a, b):
    return jnp.dot(a, b, preferred_element_type=F32)


def mm_nt(a, b):
    return lax.dot_general(a, b, (((1,), (1,)), ((), ())), preferred_element_type=F32)


def parts(value):
    high = value.astype(BF)
    return high, (value - high.astype(F32)).astype(BF)


def mm3(a_high, a_low, b):
    b_high, b_low = parts(b)
    return mm(a_high, b_high) + (mm(a_high, b_low) + mm(a_low, b_high))


def odd_rows(value, size):
    picked = [value[at : at + size] for at in range(size, value.shape[0], 2 * size)]
    return picked[0] if len(picked) == 1 else jnp.concatenate(picked, axis=0)


def put_odd_rows(value, odd, size):
    pieces = []
    for at in range(0, value.shape[0], size):
        turn = at // size
        pieces.append(
            value[at : at + size] if turn % 2 == 0 else odd[turn // 2 * size : (turn // 2 + 1) * size]
        )
    return jnp.concatenate(pieces, axis=0)


def double(tile, inverse, halves, size, apart, lower):
    high, low = halves
    width = tile.shape[1]
    link = jnp.where((lax.shift_right_logical(apart, size.bit_length() - 1) == 1) & lower, tile, 0.0)
    link = link.astype(BF)
    packed = size >= 16
    if packed:
        link = odd_rows(link, size)
        left_high, left_low = odd_rows(high, size), odd_rows(low, size)
    else:
        left_high, left_low = high, low
    if width <= 128:
        both = mm(link, jnp.concatenate([high, low], axis=1))
        inner = both[:, :width] + both[:, width:]
    else:
        inner = mm(link, high) + mm(link, low)
    if packed:
        zero = jnp.zeros((size, width), F32)
        pieces = []
        for at in range(inner.shape[0] // size):
            pieces += [zero, inner[at * size : (at + 1) * size]]
        inner = jnp.concatenate(pieces, axis=0)
    inner_high, inner_low = parts(inner)
    if width <= 128:
        rows = left_high.shape[0]
        both = mm(
            jnp.concatenate([left_high, left_low], axis=0),
            jnp.concatenate([inner_high, inner_low], axis=1),
        )
        change = both[:rows, :width] + (both[:rows, width:] + both[rows:, :width])
    else:
        change = mm(left_high, inner_high) + (mm(left_high, inner_low) + mm(left_low, inner_high))
    if packed:
        inverse = put_odd_rows(inverse, odd_rows(inverse, size) - change, size)
    else:
        inverse = inverse - change
    return inverse, parts(inverse)


def index_maps(shape):
    row = lax.broadcasted_iota(jnp.int32, shape, 0)
    col = lax.broadcasted_iota(jnp.int32, shape, 1)
    return row == col, row ^ col, row > col


def invert(tiles, pivot_rows):
    quarter = HALF // 2
    on, apart, lower = index_maps((quarter, quarter))
    small, values = [], []
    for tile, pivot in zip(tiles, pivot_rows):
        for at in range(0, HALF, quarter):
            piece = tile[at : at + quarter, at : at + quarter].astype(F32)
            across = 1.0 / pivot[:, at : at + quarter]
            diag = jnp.where(on, across, 0.0)
            down = jnp.sum(diag, axis=1, keepdims=True)
            first = jnp.where((apart == 1) & lower, piece, 0.0)
            small.append(piece)
            values.append(diag - down * first * across)
    halves = [parts(value) for value in values]
    size = 2
    while size < quarter:
        for at, piece in enumerate(small):
            values[at], halves[at] = double(piece, values[at], halves[at], size, apart, lower)
        size *= 2
    zero = jnp.zeros((quarter, quarter), F32)
    _, apart, lower = index_maps((HALF, HALF))
    result = []
    for at, tile in enumerate(tiles):
        value = jnp.concatenate(
            [
                jnp.concatenate([values[2 * at], zero], axis=1),
                jnp.concatenate([zero, values[2 * at + 1]], axis=1),
            ],
            axis=0,
        )
        result.append(double(tile.astype(F32), value, parts(value), quarter, apart, lower)[1])
    return result


def solve(tile_cross, inv, rows):
    (a_high, a_low), (b_high, b_low) = inv
    top = mm3(a_high, a_low, rows[:HALF])
    top_high, top_low = parts(top)
    rest = rows[HALF:] - (mm(tile_cross, top_high) + mm(tile_cross, top_low))
    return top.astype(BF), mm3(b_high, b_low, rest).astype(BF)


def first_kernel(slots, home_ref, factor, pivots, rows, keep, send, home, tile, pivot, value, sems):
    me = lax.axis_index("row")
    fetch_home = pltpu.make_async_copy(home_ref, home, sems.at[0])
    fetch_pivot = pltpu.make_async_copy(pivots, pivot, sems.at[1])
    fetch_home.start()
    fetch_pivot.start()
    fetch_home.wait()
    owner = home[0] // slots == me
    r0 = pl.multiple_of(home[0] % slots * BLOCK, BLOCK)
    fetch_tile = pltpu.make_async_copy(
        factor.at[pl.ds(r0, BLOCK), pl.ds(0, BLOCK)], tile, sems.at[2]
    )
    fetch_rows = pltpu.make_async_copy(rows.at[pl.ds(r0, BLOCK), :], value, sems.at[3])

    @pl.when(owner)
    def _():
        fetch_tile.start()
        fetch_rows.start()

    fetch_pivot.wait()

    @pl.when(owner)
    def _():
        fetch_tile.wait()
        pieces = [tile[h * HALF : (h + 1) * HALF, h * HALF : (h + 1) * HALF] for h in range(2)]
        inv = invert(pieces, [pivot[:, h * HALF : (h + 1) * HALF] for h in range(2)])
        fetch_rows.wait()
        top, bottom = solve(tile[HALF:, :HALF], inv, value[...])
        half = keep.shape[1]
        first = me % 2 == 0
        for at, part in enumerate((top, bottom)):
            span = slice(at * HALF, (at + 1) * HALF)
            keep[span, :] = jnp.where(first, part[:, :half], part[:, half:])
            send[span, :] = jnp.where(first, part[:, half:], part[:, :half])

    @pl.when(jnp.logical_not(owner))
    def _():
        keep[...] = jnp.zeros_like(keep)
        send[...] = jnp.zeros_like(send)


def invert_kernel(slots, home, factor, factor_there, pivots, inv_high, inv_low):
    me = lax.axis_index("row")

    def one_block(k, carry):
        r0 = pl.multiple_of(home[k] % slots * BLOCK, BLOCK)
        c0 = pl.multiple_of(k * BLOCK, BLOCK)
        for there, held in enumerate((factor, factor_there)):

            @pl.when(home[k] // slots == (me ^ there))
            def _(held=held):
                pieces = [
                    held[pl.ds(r0 + h * HALF, HALF), pl.ds(c0 + h * HALF, HALF)] for h in range(2)
                ]
                pivot_rows = [pivots[:, pl.ds(c0 + h * HALF, HALF)] for h in range(2)]
                for h, (high, low) in enumerate(invert(pieces, pivot_rows)):
                    inv_high[k - 1, h] = high
                    inv_low[k - 1, h] = low

        return carry

    lax.fori_loop(1, STEPS, one_block, 0)


def step_kernel(k, slots, home, factor, factor_there, rows, rows_there, inv_high, inv_low, *refs):
    me = lax.axis_index("row")
    solved, piece = refs[:k], refs[k]
    half = piece.shape[1]
    r0 = pl.multiple_of(home[k] % slots * BLOCK, BLOCK)
    q0 = pl.multiple_of(me % 2 * half, half)
    inv = [(inv_high.at[k - 1, h], inv_low.at[k - 1, h]) for h in range(2)]
    for there, (held, right) in enumerate(((factor, rows), (factor_there, rows_there))):

        @pl.when(home[k] // slots == (me ^ there))
        def _(held=held, right=right):
            value = right[pl.ds(r0, BLOCK), pl.ds(q0, half)]
            for j in range(k):
                value = value - mm(
                    held[pl.ds(r0, BLOCK), j * BLOCK : (j + 1) * BLOCK], solved[j][...]
                )
            cross = held[pl.ds(r0 + HALF, HALF), k * BLOCK : k * BLOCK + HALF]
            top, bottom = solve(cross, [(high[...], low[...]) for high, low in inv], value)
            piece[:HALF, :] = top
            piece[HALF:, :] = bottom

    @pl.when(home[k] // (2 * slots) != me // 2)
    def _():
        piece[...] = jnp.zeros_like(piece)


def in_order(me, mine, other):
    first = me % 2 == 0
    here, there = mine[...], other[...]
    return jnp.concatenate([jnp.where(first, here, there), jnp.where(first, there, here)], axis=1)


def columns_of(half, me, width):
    columns = half.shape[1]
    pick = (
        lax.broadcasted_iota(jnp.int32, (width, columns), 1)
        == lax.broadcasted_iota(jnp.int32, (width, columns), 0) + me * width
    ).astype(F32).astype(BF)
    return mm_nt(pick, half)


def row_of_squares(value):
    high, low = parts(value * value)
    ones = jnp.ones((8, value.shape[1]), BF)
    return (mm_nt(ones, high) + mm_nt(ones, low))[:1]


def early_kernel(k, width, factor, before, mine, other, rest, own, squares):
    me = lax.axis_index("row")
    full = in_order(me, mine, other)

    for r0 in range(0, before.shape[0], HALF):
        span = slice(r0, r0 + HALF)
        rest[span, :] = before[span, :] - mm(factor[span, k * BLOCK : (k + 1) * BLOCK], full)
    own_columns(me, width, full, own, squares)


def own_columns(me, width, full, own, squares):
    value = columns_of(full, me, width)
    own[...] = value
    squares[...] = row_of_squares(value)


def last_kernel(width, factor, rest, mine, other, out, own, squares):
    me = lax.axis_index("row")
    full = in_order(me, mine, other)
    on, _, _ = index_maps((HALF, HALF))
    eye = on.astype(F32).astype(BF)
    columns = rest.shape[1]
    for r0 in range(0, rest.shape[0], HALF):
        span = slice(r0, r0 + HALF)
        value = rest[span, :] - mm(factor[span, (STEPS - 1) * BLOCK :], full)
        value = value.astype(BF)
        for c in range(0, columns, HALF):
            out[c : c + HALF, span] = mm_nt(eye, value[:, c : c + HALF]).astype(BF)
    own_columns(me, width, full, own, squares)


def order_kernel(slots, width, home, arrived, *refs):
    owns, squares = refs[:STEPS], refs[STEPS : 2 * STEPS]
    out, variance, held, sems = refs[2 * STEPS :]
    blocks = held.shape[1] // BLOCK
    group = STEPS

    def put_out(at):
        span = pl.ds(pl.multiple_of(at * group * BLOCK, BLOCK), group * BLOCK)
        return pltpu.make_async_copy(held.at[:, span], out.at[:, span], sems.at[at])

    def place_group(at, carry):
        for turn_at in range(group):
            g = at * group + turn_at
            spot = home[g]
            r0 = pl.multiple_of((spot // slots) * width, width)
            c0 = pl.multiple_of((spot % slots) * BLOCK, BLOCK)
            o0 = pl.multiple_of(g * BLOCK, BLOCK)
            held[:, pl.ds(o0, BLOCK)] = arrived[pl.ds(r0, width), pl.ds(c0, BLOCK)].astype(F32)
        put_out(at).start()
        return carry

    total = jnp.zeros((1, width), F32)
    for j in range(STEPS):
        held[:, j * BLOCK : (j + 1) * BLOCK] = owns[j][...]
        total = total + squares[j][...]
    variance[...] = total * (1.0 / (STEPS * BLOCK))
    put_out(0).start()
    lax.fori_loop(1, blocks // group, place_group, 0)

    def drain(at, carry):
        put_out(at).wait()
        return carry

    lax.fori_loop(0, blocks // group, drain, 0)


def call(kernel, outs, in_specs, out_specs, scalars=0, scratch=(), flops=0):
    return pl.pallas_call(
        kernel,
        grid_spec=pltpu.PrefetchScalarGridSpec(
            num_scalar_prefetch=scalars,
            in_specs=in_specs,
            out_specs=out_specs,
            scratch_shapes=scratch,
        ),
        out_shape=outs,
        compiler_params=pltpu.CompilerParams(vmem_limit_bytes=VMEM_LIMIT),
        cost_estimate=pl.CostEstimate(flops=flops, bytes_accessed=0, transcendentals=0),
    )


def hop(value, count, even, odd):
    return lax.ppermute(
        value, "row", [(i, i ^ (odd if i % 2 else even)) for i in range(count)]
    )


def spread(value, count, needed, beside):
    masks = [1 << bit for bit in range(1, count.bit_length() - 1)]
    for at, mask in enumerate(masks):
        value = value + hop(value, count, mask, masks[at - 1])
        if at == 0:
            value, needed = lax.optimization_barrier((value, needed))
            done = beside(needed)
        elif at == 1:
            value, *done = lax.optimization_barrier((value, *done))
    return value, done


def on_device(factor_panel, pivots, right_sides, block_home):
    slots = factor_panel.shape[0] // BLOCK
    held_rows, columns = right_sides.shape
    count = lax.axis_size("row")
    width = columns // count
    blocks = block_home.shape[0]
    total = blocks * BLOCK
    shape = jax.ShapeDtypeStruct
    half = shape((BLOCK, columns // 2), BF)
    inverse = shape((STEPS - 1, 2, HALF, HALF), BF)
    vmem = pl.BlockSpec(memory_space=pltpu.VMEM)
    hbm = pl.BlockSpec(memory_space=pltpu.HBM)
    pivot_row = pivots.reshape(1, PANEL)
    factor_there = hop(factor_panel, count, 1, 1)
    rows_there = hop(right_sides, count, 1, 1)
    keep, send = call(
        functools.partial(first_kernel, slots),
        [half, half],
        [hbm] * 4,
        [vmem] * 2,
        scratch=(
            pltpu.SMEM((blocks,), jnp.int32),
            pltpu.VMEM((BLOCK, BLOCK), BF),
            pltpu.VMEM((1, PANEL), F32),
            pltpu.VMEM((BLOCK, columns), F32),
            pltpu.SemaphoreType.DMA((4,)),
        ),
    )(*(
        pltpu.with_memory_space_constraint(value, pltpu.HBM)
        for value in (block_home, factor_panel, pivot_row, right_sides)
    ))
    mine = keep + hop(send, count, 1, 1)
    invert_rest = call(
        functools.partial(invert_kernel, slots),
        [inverse, inverse],
        [vmem] * 3,
        [vmem] * 2,
        scalars=1,
        flops=10**9,
    )
    mine, (inv_high, inv_low) = spread(
        keep + hop(send, count, 1, 1),
        count,
        factor_there,
        lambda there: invert_rest(block_home, factor_panel, there, pivot_row),
    )
    solved = [mine]
    rest = right_sides
    owns, squares = [], []
    own_shapes = [shape((width, BLOCK), F32), shape((1, width), F32)]
    for k in range(1, STEPS):
        (piece,) = call(
            functools.partial(step_kernel, k, slots), [half], [vmem] * (6 + k), [vmem], scalars=1
        )(
            block_home, factor_panel, factor_there, right_sides, rows_there, inv_high, inv_low, *solved
        )
        piece, shared = lax.optimization_barrier((piece, solved[-1]))
        update = call(
            functools.partial(early_kernel, k - 1, width),
            [shape((held_rows, columns), F32), *own_shapes],
            [vmem] * 4,
            [vmem] * 3,
            flops=2 * held_rows * columns * BLOCK,
        )
        mine, (rest, own, square) = spread(
            piece,
            count,
            hop(shared, count, 1, 1),
            lambda other: update(factor_panel, rest, shared, other),
        )
        solved.append(mine)
        owns.append(own)
        squares.append(square)
    turned, own, square = call(
        functools.partial(last_kernel, width),
        [shape((columns, held_rows), BF), *own_shapes],
        [vmem] * 4,
        [vmem] * 3,
    )(factor_panel, rest, mine, hop(mine, count, 1, 1))
    owns.append(own)
    squares.append(square)
    arrived = lax.all_to_all(turned, "row", split_axis=0, concat_axis=0, tiled=True)
    out, variance = call(
        functools.partial(order_kernel, slots, width),
        [shape((width, total), F32), shape((1, width), F32)],
        [vmem] * (1 + 2 * STEPS),
        [hbm, vmem],
        scalars=1,
        scratch=(pltpu.VMEM((width, total), F32), pltpu.SemaphoreType.DMA((blocks // STEPS,))),
    )(block_home, arrived, *owns, *squares)
    return out.T, variance[0]


def solution(mesh):
    in_specs = (P(("groups", "row"), None), P("groups"), P(("groups", "row"), None), P())
    out_specs = (P("groups", "row"), P(("groups", "row")))
    return jax.shard_map(
        on_device, mesh=mesh, in_specs=in_specs, out_specs=out_specs, check_vma=False
    )
```

```python
import functools

import jax
import jax.numpy as jnp
from jax import lax
from jax.experimental import pallas as pl
from jax.experimental.pallas import tpu as pltpu
from jax.sharding import PartitionSpec as P

BLOCK = 512
HALF = 256
STEPS = 4
PANEL = 2048
BF = jnp.bfloat16
F32 = jnp.float32
VMEM_LIMIT = 24 * 1024 * 1024


def mm(a, b):
    return jnp.dot(a, b, preferred_element_type=F32)


def mm_nt(a, b):
    return lax.dot_general(a, b, (((1,), (1,)), ((), ())), preferred_element_type=F32)


def parts(value):
    high = value.astype(BF)
    return high, (value - high.astype(F32)).astype(BF)


def mm3(a_high, a_low, b):
    b_high, b_low = parts(b)
    return mm(a_high, b_high) + (mm(a_high, b_low) + mm(a_low, b_high))


def odd_rows(value, size):
    picked = [value[at : at + size] for at in range(size, value.shape[0], 2 * size)]
    return picked[0] if len(picked) == 1 else jnp.concatenate(picked, axis=0)


def put_odd_rows(value, odd, size):
    pieces = []
    for at in range(0, value.shape[0], size):
        turn = at // size
        pieces.append(
            value[at : at + size] if turn % 2 == 0 else odd[turn // 2 * size : (turn // 2 + 1) * size]
        )
    return jnp.concatenate(pieces, axis=0)


def double(tile, inverse, halves, size, apart, lower):
    high, low = halves
    width = tile.shape[1]
    link = jnp.where((lax.shift_right_logical(apart, size.bit_length() - 1) == 1) & lower, tile, 0.0)
    link = link.astype(BF)
    packed = size >= 16
    if packed:
        link = odd_rows(link, size)
        left_high, left_low = odd_rows(high, size), odd_rows(low, size)
    else:
        left_high, left_low = high, low
    if width <= 128:
        both = mm(link, jnp.concatenate([high, low], axis=1))
        inner = both[:, :width] + both[:, width:]
    else:
        inner = mm(link, high) + mm(link, low)
    if packed:
        zero = jnp.zeros((size, width), F32)
        pieces = []
        for at in range(inner.shape[0] // size):
            pieces += [zero, inner[at * size : (at + 1) * size]]
        inner = jnp.concatenate(pieces, axis=0)
    inner_high, inner_low = parts(inner)
    if width <= 128:
        rows = left_high.shape[0]
        both = mm(
            jnp.concatenate([left_high, left_low], axis=0),
            jnp.concatenate([inner_high, inner_low], axis=1),
        )
        change = both[:rows, :width] + (both[:rows, width:] + both[rows:, :width])
    else:
        change = mm(left_high, inner_high) + (mm(left_high, inner_low) + mm(left_low, inner_high))
    if packed:
        inverse = put_odd_rows(inverse, odd_rows(inverse, size) - change, size)
    else:
        inverse = inverse - change
    return inverse, parts(inverse)


def index_maps(shape):
    row = lax.broadcasted_iota(jnp.int32, shape, 0)
    col = lax.broadcasted_iota(jnp.int32, shape, 1)
    return row == col, row ^ col, row > col


def invert(tiles, pivot_rows):
    quarter = HALF // 2
    on, apart, lower = index_maps((quarter, quarter))
    small, values = [], []
    for tile, pivot in zip(tiles, pivot_rows):
        for at in range(0, HALF, quarter):
            piece = tile[at : at + quarter, at : at + quarter].astype(F32)
            across = 1.0 / pivot[:, at : at + quarter]
            diag = jnp.where(on, across, 0.0)
            down = jnp.sum(diag, axis=1, keepdims=True)
            first = jnp.where((apart == 1) & lower, piece, 0.0)
            small.append(piece)
            values.append(diag - down * first * across)
    halves = [parts(value) for value in values]
    size = 2
    while size < quarter:
        for at, piece in enumerate(small):
            values[at], halves[at] = double(piece, values[at], halves[at], size, apart, lower)
        size *= 2
    zero = jnp.zeros((quarter, quarter), F32)
    _, apart, lower = index_maps((HALF, HALF))
    result = []
    for at, tile in enumerate(tiles):
        value = jnp.concatenate(
            [
                jnp.concatenate([values[2 * at], zero], axis=1),
                jnp.concatenate([zero, values[2 * at + 1]], axis=1),
            ],
            axis=0,
        )
        result.append(double(tile.astype(F32), value, parts(value), quarter, apart, lower)[1])
    return result


def solve(tile_cross, inv, rows):
    (a_high, a_low), (b_high, b_low) = inv
    top = mm3(a_high, a_low, rows[:HALF])
    top_high, top_low = parts(top)
    rest = rows[HALF:] - (mm(tile_cross, top_high) + mm(tile_cross, top_low))
    return top.astype(BF), mm3(b_high, b_low, rest).astype(BF)


def first_kernel(slots, home_ref, factor, pivots, rows, keep, send, home, tile, pivot, value, sems):
    me = lax.axis_index("row")
    fetch_home = pltpu.make_async_copy(home_ref, home, sems.at[0])
    fetch_pivot = pltpu.make_async_copy(pivots, pivot, sems.at[1])
    fetch_home.start()
    fetch_pivot.start()
    fetch_home.wait()
    owner = home[0] // slots == me
    r0 = pl.multiple_of(home[0] % slots * BLOCK, BLOCK)
    fetch_tile = pltpu.make_async_copy(
        factor.at[pl.ds(r0, BLOCK), pl.ds(0, BLOCK)], tile, sems.at[2]
    )
    fetch_rows = pltpu.make_async_copy(rows.at[pl.ds(r0, BLOCK), :], value, sems.at[3])

    @pl.when(owner)
    def _():
        fetch_tile.start()
        fetch_rows.start()

    fetch_pivot.wait()

    @pl.when(owner)
    def _():
        fetch_tile.wait()
        pieces = [tile[h * HALF : (h + 1) * HALF, h * HALF : (h + 1) * HALF] for h in range(2)]
        inv = invert(pieces, [pivot[:, h * HALF : (h + 1) * HALF] for h in range(2)])
        fetch_rows.wait()
        top, bottom = solve(tile[HALF:, :HALF], inv, value[...])
        half = keep.shape[1]
        first = me % 2 == 0
        for at, part in enumerate((top, bottom)):
            span = slice(at * HALF, (at + 1) * HALF)
            keep[span, :] = jnp.where(first, part[:, :half], part[:, half:])
            send[span, :] = jnp.where(first, part[:, half:], part[:, :half])

    @pl.when(jnp.logical_not(owner))
    def _():
        keep[...] = jnp.zeros_like(keep)
        send[...] = jnp.zeros_like(send)


def invert_kernel(k, slots, home, factor, factor_there, pivots, inv_high, inv_low):
    me = lax.axis_index("row")
    r0 = pl.multiple_of(home[k] % slots * BLOCK, BLOCK)
    for there, held in enumerate((factor, factor_there)):

        @pl.when(home[k] // slots == (me ^ there))
        def _(held=held):
            spans = [slice(k * BLOCK + h * HALF, k * BLOCK + (h + 1) * HALF) for h in range(2)]
            pieces = [held[pl.ds(r0 + h * HALF, HALF), span] for h, span in enumerate(spans)]
            for h, (high, low) in enumerate(invert(pieces, [pivots[:, span] for span in spans])):
                inv_high[h] = high
                inv_low[h] = low


def step_kernel(k, slots, home, factor, factor_there, rows, rows_there, inv_high, inv_low, *refs):
    me = lax.axis_index("row")
    solved, piece = refs[:k], refs[k]
    half = piece.shape[1]
    r0 = pl.multiple_of(home[k] % slots * BLOCK, BLOCK)
    q0 = pl.multiple_of(me % 2 * half, half)
    inv = [(inv_high.at[h], inv_low.at[h]) for h in range(2)]
    for there, (held, right) in enumerate(((factor, rows), (factor_there, rows_there))):

        @pl.when(home[k] // slots == (me ^ there))
        def _(held=held, right=right):
            value = right[pl.ds(r0, BLOCK), pl.ds(q0, half)]
            for j in range(k):
                value = value - mm(
                    held[pl.ds(r0, BLOCK), j * BLOCK : (j + 1) * BLOCK], solved[j][...]
                )
            cross = held[pl.ds(r0 + HALF, HALF), k * BLOCK : k * BLOCK + HALF]
            top, bottom = solve(cross, [(high[...], low[...]) for high, low in inv], value)
            piece[:HALF, :] = top
            piece[HALF:, :] = bottom

    @pl.when(home[k] // (2 * slots) != me // 2)
    def _():
        piece[...] = jnp.zeros_like(piece)


def in_order(me, mine, other):
    first = me % 2 == 0
    here, there = mine[...], other[...]
    return jnp.concatenate([jnp.where(first, here, there), jnp.where(first, there, here)], axis=1)


def columns_of(half, me, width):
    columns = half.shape[1]
    pick = (
        lax.broadcasted_iota(jnp.int32, (width, columns), 1)
        == lax.broadcasted_iota(jnp.int32, (width, columns), 0) + me * width
    ).astype(F32).astype(BF)
    return mm_nt(pick, half)


def row_of_squares(value):
    high, low = parts(value * value)
    ones = jnp.ones((8, value.shape[1]), BF)
    return (mm_nt(ones, high) + mm_nt(ones, low))[:1]


def early_kernel(k, width, factor, before, mine, other, rest, own, squares):
    me = lax.axis_index("row")
    full = in_order(me, mine, other)

    for r0 in range(0, before.shape[0], HALF):
        span = slice(r0, r0 + HALF)
        rest[span, :] = before[span, :] - mm(factor[span, k * BLOCK : (k + 1) * BLOCK], full)
    own_columns(me, width, full, own, squares)


def own_columns(me, width, full, own, squares):
    value = columns_of(full, me, width)
    own[...] = value
    squares[...] = row_of_squares(value)


def last_kernel(width, factor, rest, mine, other, out, own, squares):
    me = lax.axis_index("row")
    full = in_order(me, mine, other)
    on, _, _ = index_maps((HALF, HALF))
    eye = on.astype(F32).astype(BF)
    columns = rest.shape[1]
    for r0 in range(0, rest.shape[0], HALF):
        span = slice(r0, r0 + HALF)
        value = rest[span, :] - mm(factor[span, (STEPS - 1) * BLOCK :], full)
        value = value.astype(BF)
        for c in range(0, columns, HALF):
            out[c : c + HALF, span] = mm_nt(eye, value[:, c : c + HALF]).astype(BF)
    own_columns(me, width, full, own, squares)


def order_kernel(slots, width, home, arrived, *refs):
    owns, squares = refs[:STEPS], refs[STEPS : 2 * STEPS]
    out, variance, held, sems = refs[2 * STEPS :]
    blocks = held.shape[1] // BLOCK
    group = STEPS

    def put_out(at):
        span = pl.ds(pl.multiple_of(at * group * BLOCK, BLOCK), group * BLOCK)
        return pltpu.make_async_copy(held.at[:, span], out.at[:, span], sems.at[at])

    def place_group(at, carry):
        for turn_at in range(group):
            g = at * group + turn_at
            spot = home[g]
            r0 = pl.multiple_of((spot // slots) * width, width)
            c0 = pl.multiple_of((spot % slots) * BLOCK, BLOCK)
            o0 = pl.multiple_of(g * BLOCK, BLOCK)
            held[:, pl.ds(o0, BLOCK)] = arrived[pl.ds(r0, width), pl.ds(c0, BLOCK)].astype(F32)
        put_out(at).start()
        return carry

    total = jnp.zeros((1, width), F32)
    for j in range(STEPS):
        held[:, j * BLOCK : (j + 1) * BLOCK] = owns[j][...]
        total = total + squares[j][...]
    variance[...] = total * (1.0 / (STEPS * BLOCK))
    put_out(0).start()
    lax.fori_loop(1, blocks // group, place_group, 0)

    def drain(at, carry):
        put_out(at).wait()
        return carry

    lax.fori_loop(0, blocks // group, drain, 0)


def call(kernel, outs, in_specs, out_specs, scalars=0, scratch=(), flops=0):
    return pl.pallas_call(
        kernel,
        grid_spec=pltpu.PrefetchScalarGridSpec(
            num_scalar_prefetch=scalars,
            in_specs=in_specs,
            out_specs=out_specs,
            scratch_shapes=scratch,
        ),
        out_shape=outs,
        compiler_params=pltpu.CompilerParams(vmem_limit_bytes=VMEM_LIMIT),
        cost_estimate=pl.CostEstimate(flops=flops, bytes_accessed=0, transcendentals=0),
    )


def hop(value, count, even, odd):
    return lax.ppermute(
        value, "row", [(i, i ^ (odd if i % 2 else even)) for i in range(count)]
    )


def orders(count):
    masks = [1 << bit for bit in range(1, count.bit_length() - 1)]
    return list(zip(masks[-1:] + masks[:-1], masks))


def spread(value, count, needed, beside, late):
    done = after = []
    for at, (even, odd) in enumerate(orders(count)):
        value = value + hop(value, count, even, odd)
        if at == 0:
            value, needed = lax.optimization_barrier((value, needed))
            done = beside(needed)
        elif at == 1:
            value, *done, needed = lax.optimization_barrier((value, *done, needed))
            after = late(needed)
        elif at == 2:
            value, *after = lax.optimization_barrier((value, *after))
    return value, done, after


def on_device(factor_panel, pivots, right_sides, block_home):
    slots = factor_panel.shape[0] // BLOCK
    held_rows, columns = right_sides.shape
    count = lax.axis_size("row")
    width = columns // count
    blocks = block_home.shape[0]
    total = blocks * BLOCK
    shape = jax.ShapeDtypeStruct
    half = shape((BLOCK, columns // 2), BF)
    inverse = shape((2, HALF, HALF), BF)
    vmem = pl.BlockSpec(memory_space=pltpu.VMEM)
    hbm = pl.BlockSpec(memory_space=pltpu.HBM)
    pivot_row = pivots.reshape(1, PANEL)
    factor_there = hop(factor_panel, count, 1, 1)
    rows_there = hop(right_sides, count, 1, 1)
    keep, send = call(
        functools.partial(first_kernel, slots),
        [half, half],
        [hbm] * 4,
        [vmem] * 2,
        scratch=(
            pltpu.SMEM((blocks,), jnp.int32),
            pltpu.VMEM((BLOCK, BLOCK), BF),
            pltpu.VMEM((1, PANEL), F32),
            pltpu.VMEM((BLOCK, columns), F32),
            pltpu.SemaphoreType.DMA((4,)),
        ),
    )(*(
        pltpu.with_memory_space_constraint(value, pltpu.HBM)
        for value in (block_home, factor_panel, pivot_row, right_sides)
    ))
    mine = keep + hop(send, count, 1, 1)

    def invert_block(k):
        return lambda there: call(
            functools.partial(invert_kernel, k, slots),
            [inverse, inverse],
            [vmem] * 3,
            [vmem] * 2,
            scalars=1,
            flops=5 * 10**8,
        )(block_home, factor_panel, there, pivot_row)

    mine, *inverses = spread(
        keep + hop(send, count, 1, 1), count, factor_there, invert_block(1), invert_block(2)
    )
    solved = [mine]
    rest = right_sides
    owns, squares = [], []
    own_shapes = [shape((width, BLOCK), F32), shape((1, width), F32)]
    for k in range(1, STEPS):
        (piece,) = call(
            functools.partial(step_kernel, k, slots), [half], [vmem] * (6 + k), [vmem], scalars=1
        )(
            block_home,
            factor_panel,
            factor_there,
            right_sides,
            rows_there,
            *inverses[k - 1],
            *solved,
        )
        piece, shared = lax.optimization_barrier((piece, solved[-1]))
        update = call(
            functools.partial(early_kernel, k - 1, width),
            [shape((held_rows, columns), F32), *own_shapes],
            [vmem] * 4,
            [vmem] * 3,
            flops=2 * held_rows * columns * BLOCK,
        )
        mine, (rest, own, square), inverse_next = spread(
            piece,
            count,
            hop(shared, count, 1, 1),
            lambda other: update(factor_panel, rest, shared, other),
            lambda _: invert_block(3)(factor_there) if k == 1 else [],
        )
        inverses.append(inverse_next)
        solved.append(mine)
        owns.append(own)
        squares.append(square)
    turned, own, square = call(
        functools.partial(last_kernel, width),
        [shape((columns, held_rows), BF), *own_shapes],
        [vmem] * 4,
        [vmem] * 3,
    )(factor_panel, rest, mine, hop(mine, count, 1, 1))
    owns.append(own)
    squares.append(square)
    arrived = lax.all_to_all(turned, "row", split_axis=0, concat_axis=0, tiled=True)
    out, variance = call(
        functools.partial(order_kernel, slots, width),
        [shape((width, total), F32), shape((1, width), F32)],
        [vmem] * (1 + 2 * STEPS),
        [hbm, vmem],
        scalars=1,
        scratch=(pltpu.VMEM((width, total), F32), pltpu.SemaphoreType.DMA((blocks // STEPS,))),
    )(block_home, arrived, *owns, *squares)
    return out.T, variance[0]


def solution(mesh):
    in_specs = (P(("groups", "row"), None), P("groups"), P(("groups", "row"), None), P())
    out_specs = (P("groups", "row"), P(("groups", "row")))
    return jax.shard_map(
        on_device, mesh=mesh, in_specs=in_specs, out_specs=out_specs, check_vma=False
    )
```

```python
import functools

import jax
import jax.numpy as jnp
from jax import lax
from jax.experimental import pallas as pl
from jax.experimental.pallas import tpu as pltpu
from jax.sharding import PartitionSpec as P

BLOCK = 512
HALF = 256
STEPS = 4
PANEL = 2048
BF = jnp.bfloat16
F32 = jnp.float32
VMEM_LIMIT = 24 * 1024 * 1024


def mm(a, b):
    return jnp.dot(a, b, preferred_element_type=F32)


def mm_nt(a, b):
    return lax.dot_general(a, b, (((1,), (1,)), ((), ())), preferred_element_type=F32)


def parts(value):
    high = value.astype(BF)
    return high, (value - high.astype(F32)).astype(BF)


def mm3(a_high, a_low, b):
    b_high, b_low = parts(b)
    return mm(a_high, b_high) + (mm(a_high, b_low) + mm(a_low, b_high))


def odd_rows(value, size):
    picked = [value[at : at + size] for at in range(size, value.shape[0], 2 * size)]
    return picked[0] if len(picked) == 1 else jnp.concatenate(picked, axis=0)


def put_odd_rows(value, odd, size):
    pieces = []
    for at in range(0, value.shape[0], size):
        turn = at // size
        pieces.append(
            value[at : at + size] if turn % 2 == 0 else odd[turn // 2 * size : (turn // 2 + 1) * size]
        )
    return jnp.concatenate(pieces, axis=0)


def double(tile, inverse, halves, size, apart, lower):
    high, low = halves
    width = tile.shape[1]
    link = jnp.where((lax.shift_right_logical(apart, size.bit_length() - 1) == 1) & lower, tile, 0.0)
    link = link.astype(BF)
    packed = size >= 16
    if packed:
        link = odd_rows(link, size)
        left_high, left_low = odd_rows(high, size), odd_rows(low, size)
    else:
        left_high, left_low = high, low
    if width <= 128:
        both = mm(link, jnp.concatenate([high, low], axis=1))
        inner = both[:, :width] + both[:, width:]
    else:
        inner = mm(link, high) + mm(link, low)
    if packed:
        zero = jnp.zeros((size, width), F32)
        pieces = []
        for at in range(inner.shape[0] // size):
            pieces += [zero, inner[at * size : (at + 1) * size]]
        inner = jnp.concatenate(pieces, axis=0)
    inner_high, inner_low = parts(inner)
    if width <= 128:
        rows = left_high.shape[0]
        both = mm(
            jnp.concatenate([left_high, left_low], axis=0),
            jnp.concatenate([inner_high, inner_low], axis=1),
        )
        change = both[:rows, :width] + (both[:rows, width:] + both[rows:, :width])
    else:
        change = mm(left_high, inner_high) + (mm(left_high, inner_low) + mm(left_low, inner_high))
    if packed:
        inverse = put_odd_rows(inverse, odd_rows(inverse, size) - change, size)
    else:
        inverse = inverse - change
    return inverse, parts(inverse)


def index_maps(shape):
    row = lax.broadcasted_iota(jnp.int32, shape, 0)
    col = lax.broadcasted_iota(jnp.int32, shape, 1)
    return row == col, row ^ col, row > col


def eight_by_eight(piece, across, down):
    width = piece.shape[1]
    lane = lax.broadcasted_iota(jnp.int32, (8, width), 1)
    row = lax.broadcasted_iota(jnp.int32, (8, width), 0)
    block, col = lax.shift_right_logical(lane, 3), lane & 7
    held = jnp.zeros((8, width), F32)
    for b in range(width // 8):
        held = jnp.where(block == b, piece[8 * b : 8 * b + 8], held)
    held = jnp.where(row > col, held, 0.0) * across
    unit = jnp.where(row == col, 1.0, 0.0).astype(F32)
    for j in range(7):
        factor = jnp.where(col == j, held, 0.0)
        if j:
            factor = pltpu.roll(factor, width - j, 1)
        for shift in (1, 2, 4):
            factor = factor + pltpu.roll(factor, shift, 1)
        unit = unit - factor * unit[j : j + 1]
    spread_out = [jnp.where(block == b, unit, 0.0) for b in range(width // 8)]
    return jnp.concatenate(spread_out, axis=0) * down


def invert(tiles, pivot_rows):
    quarter = HALF // 2
    on, apart, lower = index_maps((quarter, quarter))
    small, values = [], []
    for tile, pivot in zip(tiles, pivot_rows):
        for at in range(0, HALF, quarter):
            piece = tile[at : at + quarter, at : at + quarter].astype(F32)
            across = 1.0 / pivot[:, at : at + quarter]
            down = jnp.sum(jnp.where(on, across, 0.0), axis=1, keepdims=True)
            small.append(piece)
            values.append(eight_by_eight(piece, across, down))
    halves = [parts(value) for value in values]
    size = 8
    while size < quarter:
        for at, piece in enumerate(small):
            values[at], halves[at] = double(piece, values[at], halves[at], size, apart, lower)
        size *= 2
    zero = jnp.zeros((quarter, quarter), F32)
    _, apart, lower = index_maps((HALF, HALF))
    result = []
    for at, tile in enumerate(tiles):
        value = jnp.concatenate(
            [
                jnp.concatenate([values[2 * at], zero], axis=1),
                jnp.concatenate([zero, values[2 * at + 1]], axis=1),
            ],
            axis=0,
        )
        result.append(double(tile.astype(F32), value, parts(value), quarter, apart, lower)[1])
    return result


def solve(tile_cross, inv, rows):
    (a_high, a_low), (b_high, b_low) = inv
    top = mm3(a_high, a_low, rows[:HALF])
    top_high, top_low = parts(top)
    rest = rows[HALF:] - (mm(tile_cross, top_high) + mm(tile_cross, top_low))
    return top.astype(BF), mm3(b_high, b_low, rest).astype(BF)


def first_kernel(slots, home_ref, factor, pivots, rows, keep, send, home, tile, pivot, value, sems):
    me = lax.axis_index("row")
    fetch_home = pltpu.make_async_copy(home_ref, home, sems.at[0])
    fetch_pivot = pltpu.make_async_copy(pivots, pivot, sems.at[1])
    fetch_tile = pltpu.make_async_copy(factor.at[:, pl.ds(0, BLOCK)], tile, sems.at[2])
    fetch_rows = pltpu.make_async_copy(rows, value, sems.at[3])
    fetch_home.start()
    fetch_tile.start()
    fetch_pivot.start()
    fetch_rows.start()
    fetch_home.wait()
    owner = home[0] // slots == me
    r0 = pl.multiple_of(home[0] % slots * BLOCK, BLOCK)
    fetch_pivot.wait()
    fetch_tile.wait()
    fetch_rows.wait()

    @pl.when(owner)
    def _():
        pieces = [
            tile[pl.ds(r0 + h * HALF, HALF), h * HALF : (h + 1) * HALF] for h in range(2)
        ]
        inv = invert(pieces, [pivot[:, h * HALF : (h + 1) * HALF] for h in range(2)])
        cross = tile[pl.ds(r0 + HALF, HALF), :HALF]
        top, bottom = solve(cross, inv, value[pl.ds(r0, BLOCK), :])
        half = keep.shape[1]
        first = me % 2 == 0
        for at, part in enumerate((top, bottom)):
            span = slice(at * HALF, (at + 1) * HALF)
            keep[span, :] = jnp.where(first, part[:, :half], part[:, half:])
            send[span, :] = jnp.where(first, part[:, half:], part[:, :half])

    @pl.when(jnp.logical_not(owner))
    def _():
        keep[...] = jnp.zeros_like(keep)
        send[...] = jnp.zeros_like(send)


def invert_kernel(k, slots, home, factor, factor_there, pivots, inv_high, inv_low):
    me = lax.axis_index("row")
    r0 = pl.multiple_of(home[k] % slots * BLOCK, BLOCK)
    for there, held in enumerate((factor, factor_there)):

        @pl.when(home[k] // slots == (me ^ there))
        def _(held=held):
            spans = [slice(k * BLOCK + h * HALF, k * BLOCK + (h + 1) * HALF) for h in range(2)]
            pieces = [held[pl.ds(r0 + h * HALF, HALF), span] for h, span in enumerate(spans)]
            for h, (high, low) in enumerate(invert(pieces, [pivots[:, span] for span in spans])):
                inv_high[h] = high
                inv_low[h] = low


def step_kernel(k, slots, home, factor, factor_there, rows, rows_there, inv_high, inv_low, *refs):
    me = lax.axis_index("row")
    solved, piece = refs[:k], refs[k]
    half = piece.shape[1]
    r0 = pl.multiple_of(home[k] % slots * BLOCK, BLOCK)
    q0 = pl.multiple_of(me % 2 * half, half)
    inv = [(inv_high.at[h], inv_low.at[h]) for h in range(2)]
    for there, (held, right) in enumerate(((factor, rows), (factor_there, rows_there))):

        @pl.when(home[k] // slots == (me ^ there))
        def _(held=held, right=right):
            value = right[pl.ds(r0, BLOCK), pl.ds(q0, half)]
            for j in range(k):
                value = value - mm(
                    held[pl.ds(r0, BLOCK), j * BLOCK : (j + 1) * BLOCK], solved[j][...]
                )
            cross = held[pl.ds(r0 + HALF, HALF), k * BLOCK : k * BLOCK + HALF]
            top, bottom = solve(cross, [(high[...], low[...]) for high, low in inv], value)
            piece[:HALF, :] = top
            piece[HALF:, :] = bottom

    @pl.when(home[k] // (2 * slots) != me // 2)
    def _():
        piece[...] = jnp.zeros_like(piece)


def in_order(me, mine, other):
    first = me % 2 == 0
    here, there = mine[...], other[...]
    return jnp.concatenate([jnp.where(first, here, there), jnp.where(first, there, here)], axis=1)


def columns_of(half, me, width):
    columns = half.shape[1]
    pick = (
        lax.broadcasted_iota(jnp.int32, (width, columns), 1)
        == lax.broadcasted_iota(jnp.int32, (width, columns), 0) + me * width
    ).astype(F32).astype(BF)
    return mm_nt(pick, half)


def row_of_squares(value):
    high, low = parts(value * value)
    ones = jnp.ones((8, value.shape[1]), BF)
    return (mm_nt(ones, high) + mm_nt(ones, low))[:1]


def early_kernel(k, width, factor, before, mine, other, rest, own, squares):
    me = lax.axis_index("row")
    full = in_order(me, mine, other)

    for r0 in range(0, before.shape[0], HALF):
        span = slice(r0, r0 + HALF)
        rest[span, :] = before[span, :] - mm(factor[span, k * BLOCK : (k + 1) * BLOCK], full)
    own_columns(me, width, full, own, squares)


def own_columns(me, width, full, own, squares):
    value = columns_of(full, me, width)
    own[...] = value
    squares[...] = row_of_squares(value)


def last_kernel(width, factor, rest, mine, other, out, own, squares):
    me = lax.axis_index("row")
    full = in_order(me, mine, other)
    on, _, _ = index_maps((HALF, HALF))
    eye = on.astype(F32).astype(BF)
    columns = rest.shape[1]
    for r0 in range(0, rest.shape[0], HALF):
        span = slice(r0, r0 + HALF)
        value = rest[span, :] - mm(factor[span, (STEPS - 1) * BLOCK :], full)
        value = value.astype(BF)
        for c in range(0, columns, HALF):
            out[c : c + HALF, span] = mm_nt(eye, value[:, c : c + HALF]).astype(BF)
    own_columns(me, width, full, own, squares)


def order_kernel(slots, width, home, arrived, *refs):
    owns, squares = refs[:STEPS], refs[STEPS : 2 * STEPS]
    out, variance, held, sems = refs[2 * STEPS :]
    blocks = held.shape[1] // BLOCK
    group = STEPS

    def put_out(at):
        span = pl.ds(pl.multiple_of(at * group * BLOCK, BLOCK), group * BLOCK)
        return pltpu.make_async_copy(held.at[:, span], out.at[:, span], sems.at[at])

    def place_group(at, carry):
        for turn_at in range(group):
            g = at * group + turn_at
            spot = home[g]
            r0 = pl.multiple_of((spot // slots) * width, width)
            c0 = pl.multiple_of((spot % slots) * BLOCK, BLOCK)
            o0 = pl.multiple_of(g * BLOCK, BLOCK)
            held[:, pl.ds(o0, BLOCK)] = arrived[pl.ds(r0, width), pl.ds(c0, BLOCK)].astype(F32)
        put_out(at).start()
        return carry

    total = jnp.zeros((1, width), F32)
    for j in range(STEPS):
        held[:, j * BLOCK : (j + 1) * BLOCK] = owns[j][...]
        total = total + squares[j][...]
    variance[...] = total * (1.0 / (STEPS * BLOCK))
    put_out(0).start()
    lax.fori_loop(1, blocks // group, place_group, 0)

    def drain(at, carry):
        put_out(at).wait()
        return carry

    lax.fori_loop(0, blocks // group, drain, 0)


def call(kernel, outs, in_specs, out_specs, scalars=0, scratch=(), flops=0):
    return pl.pallas_call(
        kernel,
        grid_spec=pltpu.PrefetchScalarGridSpec(
            num_scalar_prefetch=scalars,
            in_specs=in_specs,
            out_specs=out_specs,
            scratch_shapes=scratch,
        ),
        out_shape=outs,
        compiler_params=pltpu.CompilerParams(vmem_limit_bytes=VMEM_LIMIT),
        cost_estimate=pl.CostEstimate(flops=flops, bytes_accessed=0, transcendentals=0),
    )


def hop(value, count, even, odd):
    return lax.ppermute(
        value, "row", [(i, i ^ (odd if i % 2 else even)) for i in range(count)]
    )


def orders(count):
    masks = [1 << bit for bit in range(1, count.bit_length() - 1)]
    return list(zip(masks[-1:] + masks[:-1], masks))


def spread(value, count, needed, beside, late):
    done = after = []
    for at, (even, odd) in enumerate(orders(count)):
        value = value + hop(value, count, even, odd)
        if at == 0 and beside:
            value, needed = lax.optimization_barrier((value, needed))
            done = beside(needed)
        elif at == 1:
            value, *done, needed = lax.optimization_barrier((value, *done, needed))
            after = late(needed)
        elif at == 2:
            value, *after = lax.optimization_barrier((value, *after))
    return value, done, after


def on_device(factor_panel, pivots, right_sides, block_home):
    slots = factor_panel.shape[0] // BLOCK
    held_rows, columns = right_sides.shape
    count = lax.axis_size("row")
    width = columns // count
    blocks = block_home.shape[0]
    total = blocks * BLOCK
    shape = jax.ShapeDtypeStruct
    half = shape((BLOCK, columns // 2), BF)
    inverse = shape((2, HALF, HALF), BF)
    vmem = pl.BlockSpec(memory_space=pltpu.VMEM)
    hbm = pl.BlockSpec(memory_space=pltpu.HBM)
    pivot_row = pivots.reshape(1, PANEL)
    keep, send = call(
        functools.partial(first_kernel, slots),
        [half, half],
        [hbm] * 4,
        [vmem] * 2,
        scratch=(
            pltpu.SMEM((blocks,), jnp.int32),
            pltpu.VMEM((held_rows, BLOCK), BF),
            pltpu.VMEM((1, PANEL), F32),
            pltpu.VMEM((held_rows, columns), F32),
            pltpu.SemaphoreType.DMA((4,)),
        ),
    )(*(
        pltpu.with_memory_space_constraint(value, pltpu.HBM)
        for value in (block_home, factor_panel, pivot_row, right_sides)
    ))
    mine = keep + hop(send, count, 1, 1)

    def invert_block(k):
        return lambda there: call(
            functools.partial(invert_kernel, k, slots),
            [inverse, inverse],
            [vmem] * 3,
            [vmem] * 2,
            scalars=1,
            flops=5 * 10**8,
        )(block_home, factor_panel, there, pivot_row)

    mine, rows_sent, factor_sent = lax.optimization_barrier(
        (keep + hop(send, count, 1, 1), right_sides, factor_panel)
    )
    factor_there = hop(factor_sent, count, 1, 1)
    rows_there = hop(rows_sent, count, 1, 1)
    mine, _, inverse_next = spread(mine, count, factor_there, None, invert_block(1))
    inverses = [inverse_next]
    solved = [mine]
    rest = right_sides
    owns, squares = [], []
    own_shapes = [shape((width, BLOCK), F32), shape((1, width), F32)]
    for k in range(1, STEPS):
        (piece,) = call(
            functools.partial(step_kernel, k, slots), [half], [vmem] * (6 + k), [vmem], scalars=1
        )(
            block_home,
            factor_panel,
            factor_there,
            right_sides,
            rows_there,
            *inverses[k - 1],
            *solved,
        )
        piece, shared = lax.optimization_barrier((piece, solved[-1]))
        update = call(
            functools.partial(early_kernel, k - 1, width),
            [shape((held_rows, columns), F32), *own_shapes],
            [vmem] * 4,
            [vmem] * 3,
            flops=2 * held_rows * columns * BLOCK,
        )
        mine, (rest, own, square), inverse_next = spread(
            piece,
            count,
            hop(shared, count, 1, 1),
            lambda other: update(factor_panel, rest, shared, other),
            lambda _: invert_block(k + 1)(factor_there) if k + 1 < STEPS else [],
        )
        inverses.append(inverse_next)
        solved.append(mine)
        owns.append(own)
        squares.append(square)
    turned, own, square = call(
        functools.partial(last_kernel, width),
        [shape((columns, held_rows), BF), *own_shapes],
        [vmem] * 4,
        [vmem] * 3,
    )(factor_panel, rest, mine, hop(mine, count, 1, 1))
    owns.append(own)
    squares.append(square)
    arrived = lax.all_to_all(turned, "row", split_axis=0, concat_axis=0, tiled=True)
    out, variance = call(
        functools.partial(order_kernel, slots, width),
        [shape((width, total), F32), shape((1, width), F32)],
        [vmem] * (1 + 2 * STEPS),
        [hbm, vmem],
        scalars=1,
        scratch=(pltpu.VMEM((width, total), F32), pltpu.SemaphoreType.DMA((blocks // STEPS,))),
    )(block_home, arrived, *owns, *squares)
    return out.T, variance[0]


def solution(mesh):
    in_specs = (P(("groups", "row"), None), P("groups"), P(("groups", "row"), None), P())
    out_specs = (P("groups", "row"), P(("groups", "row")))
    return jax.shard_map(
        on_device, mesh=mesh, in_specs=in_specs, out_specs=out_specs, check_vma=False
    )
```

```python
import functools

import jax
import jax.numpy as jnp
from jax import lax
from jax.experimental import pallas as pl
from jax.experimental.pallas import tpu as pltpu
from jax.sharding import PartitionSpec as P

BLOCK = 512
HALF = 256
STEPS = 4
START = 16
PANEL = 2048
BF = jnp.bfloat16
F32 = jnp.float32
VMEM_LIMIT = 24 * 1024 * 1024


def mm(a, b):
    return jnp.dot(a, b, preferred_element_type=F32)


def mm_nt(a, b):
    return lax.dot_general(a, b, (((1,), (1,)), ((), ())), preferred_element_type=F32)


def parts(value):
    high = value.astype(BF)
    return high, (value - high.astype(F32)).astype(BF)


def mm3(a_high, a_low, b):
    b_high, b_low = parts(b)
    rows, width = a_high.shape[0], b.shape[1]
    if width <= 128:
        both = mm(jnp.concatenate([a_high, a_low]), jnp.concatenate([b_high, b_low], axis=1))
        return both[:rows, :width] + (both[:rows, width:] + both[rows:, :width])
    return mm(a_high, b_high) + (mm(a_high, b_low) + mm(a_low, b_high))


def mm2(a, b):
    b_high, b_low = parts(b)
    width = b.shape[1]
    if width <= 128:
        both = mm(a, jnp.concatenate([b_high, b_low], axis=1))
        return both[:, :width] + both[:, width:]
    return mm(a, b_high) + mm(a, b_low)


def odd_rows(value, size):
    picked = [value[at : at + size] for at in range(size, value.shape[0], 2 * size)]
    return picked[0] if len(picked) == 1 else jnp.concatenate(picked, axis=0)


def put_odd_rows(value, odd, size):
    pieces = []
    for at in range(0, value.shape[0], size):
        turn = at // size
        pieces.append(
            value[at : at + size] if turn % 2 == 0 else odd[turn // 2 * size : (turn // 2 + 1) * size]
        )
    return jnp.concatenate(pieces, axis=0)


def double(tile, inverse, halves, size, apart, lower):
    high, low = halves
    width = tile.shape[1]
    link = jnp.where((lax.shift_right_logical(apart, size.bit_length() - 1) == 1) & lower, tile, 0.0)
    link = link.astype(BF)
    packed = size >= 16
    if packed:
        link = odd_rows(link, size)
        left_high, left_low = odd_rows(high, size), odd_rows(low, size)
    else:
        left_high, left_low = high, low
    if width <= 128:
        both = mm(link, jnp.concatenate([high, low], axis=1))
        inner = both[:, :width] + both[:, width:]
    else:
        inner = mm(link, high) + mm(link, low)
    if packed:
        zero = jnp.zeros((size, width), F32)
        pieces = []
        for at in range(inner.shape[0] // size):
            pieces += [zero, inner[at * size : (at + 1) * size]]
        inner = jnp.concatenate(pieces, axis=0)
    inner_high, inner_low = parts(inner)
    if width <= 128:
        rows = left_high.shape[0]
        both = mm(
            jnp.concatenate([left_high, left_low], axis=0),
            jnp.concatenate([inner_high, inner_low], axis=1),
        )
        change = both[:rows, :width] + (both[:rows, width:] + both[rows:, :width])
    else:
        change = mm(left_high, inner_high) + (mm(left_high, inner_low) + mm(left_low, inner_high))
    if packed:
        inverse = put_odd_rows(inverse, odd_rows(inverse, size) - change, size)
    else:
        inverse = inverse - change
    return inverse, parts(inverse)


def index_maps(shape):
    row = lax.broadcasted_iota(jnp.int32, shape, 0)
    col = lax.broadcasted_iota(jnp.int32, shape, 1)
    return row == col, row ^ col, row > col


def start_blocks(piece, across, down):
    width = piece.shape[1]
    shape = (START, width)
    lane = lax.broadcasted_iota(jnp.int32, shape, 1)
    row = lax.broadcasted_iota(jnp.int32, shape, 0)
    block, col = lax.shift_right_logical(lane, START.bit_length() - 1), lane & (START - 1)
    held = jnp.zeros(shape, F32)
    for b in range(width // START):
        held = jnp.where(block == b, piece[START * b : START * (b + 1)], held)
    held = jnp.where(row > col, held, 0.0) * across
    unit = jnp.where(row == col, 1.0, 0.0).astype(F32)
    for j in range(START - 1):
        factor = jnp.where(col == j, held, 0.0)
        if j:
            factor = pltpu.roll(factor, width - j, 1)
        shift = 1
        while shift < START:
            factor = factor + pltpu.roll(factor, shift, 1)
            shift *= 2
        unit = unit - factor * unit[j : j + 1]
    spread_out = [jnp.where(block == b, unit, 0.0) for b in range(width // START)]
    return jnp.concatenate(spread_out, axis=0) * down


def invert(tiles, pivot_rows):
    quarter = HALF // 2
    on, apart, lower = index_maps((quarter, quarter))
    small, values = [], []
    for tile, pivot in zip(tiles, pivot_rows):
        for at in range(0, HALF, quarter):
            piece = tile[at : at + quarter, at : at + quarter].astype(F32)
            across = 1.0 / pivot[:, at : at + quarter]
            down = jnp.sum(jnp.where(on, across, 0.0), axis=1, keepdims=True)
            small.append(piece)
            values.append(start_blocks(piece, across, down))
    halves = [parts(value) for value in values]
    size = START
    while size < quarter:
        for at, piece in enumerate(small):
            values[at], halves[at] = double(piece, values[at], halves[at], size, apart, lower)
        size *= 2
    zero = jnp.zeros((quarter, quarter), F32)
    _, apart, lower = index_maps((HALF, HALF))
    result = []
    for at, tile in enumerate(tiles):
        value = jnp.concatenate(
            [
                jnp.concatenate([values[2 * at], zero], axis=1),
                jnp.concatenate([zero, values[2 * at + 1]], axis=1),
            ],
            axis=0,
        )
        result.append(double(tile.astype(F32), value, parts(value), quarter, apart, lower)[1])
    return result


def solve(tile_cross, inv, rows):
    top = mm3(*inv[0], rows[:HALF])
    bottom = mm3(*inv[1], rows[HALF:] - mm2(tile_cross, top))
    return top.astype(BF), bottom.astype(BF)


def pick_columns(columns, width, parity):
    shape = (columns, columns // 2)
    row = lax.broadcasted_iota(jnp.int32, shape, 0)
    col = lax.broadcasted_iota(jnp.int32, shape, 1)
    bits = width.bit_length() - 1
    group = lax.shift_right_logical(col, bits)
    wanted = (2 * group + parity) * width + (col & (width - 1))
    return jnp.where(row == wanted, 1.0, 0.0).astype(BF)


def picked(value, chosen):
    high = value.astype(BF)
    rest = value - high.astype(F32)
    middle, low = parts(rest)
    return mm(high, chosen) + (mm(middle, chosen) + mm(low, chosen))


def first_kernel(slots, width, home_ref, factor, pivots, rows, keep, send, home, tile, pivot, value, sems):
    me = lax.axis_index("row")
    fetch_home = pltpu.make_async_copy(home_ref, home, sems.at[0])
    fetch_pivot = pltpu.make_async_copy(pivots, pivot, sems.at[1])
    fetch_tile = pltpu.make_async_copy(factor.at[:, pl.ds(0, BLOCK)], tile, sems.at[2])
    fetch_rows = pltpu.make_async_copy(rows, value, sems.at[3])
    fetch_home.start()
    fetch_tile.start()
    fetch_pivot.start()
    fetch_rows.start()
    fetch_home.wait()
    owner = home[0] // slots == me
    r0 = pl.multiple_of(home[0] % slots * BLOCK, BLOCK)
    fetch_pivot.wait()
    fetch_tile.wait()
    fetch_rows.wait()

    @pl.when(owner)
    def _():
        pieces = [
            tile[pl.ds(r0 + h * HALF, HALF), h * HALF : (h + 1) * HALF] for h in range(2)
        ]
        inv = invert(pieces, [pivot[:, h * HALF : (h + 1) * HALF] for h in range(2)])
        cross = tile[pl.ds(r0 + HALF, HALF), :HALF]
        top, bottom = solve(cross, inv, value[pl.ds(r0, BLOCK), :])
        here = pick_columns(rows.shape[1], width, me % 2)
        there = pick_columns(rows.shape[1], width, 1 - me % 2)
        for at, part in enumerate((top, bottom)):
            span = slice(at * HALF, (at + 1) * HALF)
            keep[span, :] = mm(part, here).astype(BF)
            send[span, :] = mm(part, there).astype(BF)

    @pl.when(jnp.logical_not(owner))
    def _():
        keep[...] = jnp.zeros_like(keep)
        send[...] = jnp.zeros_like(send)


def ready_kernel(k, slots, width, home, factor, factor_there, pivots, rows, rows_there, *refs):
    solved, (weights, cross, start) = refs[: k - 1], refs[k - 1 :]
    me = lax.axis_index("row")
    r0 = pl.multiple_of(home[k] % slots * BLOCK, BLOCK)
    for there, (held, right) in enumerate(((factor, rows), (factor_there, rows_there))):

        @pl.when(home[k] // slots == (me ^ there))
        def _(held=held, right=right):
            spans = [slice(k * BLOCK + h * HALF, k * BLOCK + (h + 1) * HALF) for h in range(2)]
            pieces = [held[pl.ds(r0 + h * HALF, HALF), span] for h, span in enumerate(spans)]
            inv = invert(pieces, [pivots[:, span] for span in spans])
            chosen = pick_columns(right.shape[1], width, me % 2)
            value = picked(right[pl.ds(r0, BLOCK), :], chosen)
            for j in range(k - 1):
                value = value - mm(
                    held[pl.ds(r0, BLOCK), j * BLOCK : (j + 1) * BLOCK], solved[j][...]
                )
            for h, (high, low) in enumerate(inv):
                span = slice(h * HALF, (h + 1) * HALF)
                low_span = slice(BLOCK + h * HALF, BLOCK + (h + 1) * HALF)
                left = held[pl.ds(r0 + h * HALF, HALF), (k - 1) * BLOCK : k * BLOCK]
                weights[span, :], weights[low_span, :] = parts(mm(high, left) + mm(low, left))
                start[span, :] = mm3(high, low, value[span])
            high, low = inv[1]
            link = held[pl.ds(r0 + HALF, HALF), spans[0]]
            cross[:HALF, :], cross[HALF:, :] = parts(mm(high, link) + mm(low, link))


def step_kernel(k, slots, home, weights, cross, start, before, arrived, piece, whole):
    me = lax.axis_index("row")
    previous = before[...] + arrived[...]
    whole[...] = previous
    owner = home[k] // (2 * slots) == me // 2

    @pl.when(owner)
    def _():
        both = mm(weights[...], previous)
        value = start[...] - (both[:BLOCK] + both[BLOCK:])
        top = value[:HALF]
        piece[:HALF, :] = top.astype(BF)
        piece[HALF:, :] = (value[HALF:] - mm3(cross[:HALF, :], cross[HALF:, :], top)).astype(BF)

    @pl.when(jnp.logical_not(owner))
    def _():
        piece[...] = jnp.zeros_like(piece)


def columns_of(half, at, width):
    shape = (width, half.shape[1])
    pick = (
        lax.broadcasted_iota(jnp.int32, shape, 1)
        == lax.broadcasted_iota(jnp.int32, shape, 0) + at * width
    ).astype(F32).astype(BF)
    return mm_nt(pick, half)


def row_of_squares(value):
    high, low = parts(value * value)
    ones = jnp.ones((8, value.shape[1]), BF)
    return (mm_nt(ones, high) + mm_nt(ones, low))[:1]


def early_kernel(k, width, factor, factor_there, *refs):
    before, (solved, rest, own, squares) = refs[:-4], refs[-4:]
    me = lax.axis_index("row")
    full = solved[...]
    held_rows = factor.shape[0]
    for at, held in enumerate((factor, factor_there)):
        for r0 in range(0, held_rows, HALF):
            span = slice(at * held_rows + r0, at * held_rows + r0 + HALF)
            here = slice(r0, r0 + HALF)
            if k == 0:
                right = before[at]
                value = picked(right[here, :], pick_columns(right.shape[1], width, me % 2))
            else:
                value = before[0][span, :]
            rest[span, :] = value - mm(held[here, k * BLOCK : (k + 1) * BLOCK], full)
    own_columns(me // 2, width, full, own, squares)


def own_columns(at, width, full, own, squares):
    value = columns_of(full, at, width)
    own[...] = value
    squares[...] = row_of_squares(value)


def last_kernel(width, factor, factor_there, rest, before, arrived, out, own, squares):
    me = lax.axis_index("row")
    full = before[...] + arrived[...]
    columns = rest.shape[1]
    size = min(HALF, columns)
    on, _, _ = index_maps((size, size))
    eye = on.astype(F32).astype(BF)
    held_rows = factor.shape[0]
    for at, held in enumerate((factor, factor_there)):
        place = pl.multiple_of((me % 2 ^ at) * held_rows, held_rows)
        for r0 in range(0, held_rows, HALF):
            value = rest[at * held_rows + r0 : at * held_rows + r0 + HALF, :]
            value = value - mm(held[r0 : r0 + HALF, (STEPS - 1) * BLOCK :], full)
            value = value.astype(BF)
            for c in range(0, columns, size):
                out[c : c + size, pl.ds(place + r0, HALF)] = mm_nt(
                    eye, value[:, c : c + size]
                ).astype(BF)
    own_columns(me // 2, width, full, own, squares)


def order_kernel(slots, width, home, arrived, *refs):
    owns, squares = refs[:STEPS], refs[STEPS : 2 * STEPS]
    out, variance, held, sems = refs[2 * STEPS :]
    blocks = held.shape[1] // BLOCK
    group = STEPS

    def put_out(at):
        span = pl.ds(pl.multiple_of(at * group * BLOCK, BLOCK), group * BLOCK)
        return pltpu.make_async_copy(held.at[:, span], out.at[:, span], sems.at[at])

    def place_group(at, carry):
        for turn_at in range(group):
            g = at * group + turn_at
            spot = home[g]
            r0 = pl.multiple_of(spot // (2 * slots) * width, width)
            c0 = pl.multiple_of(spot % (2 * slots) * BLOCK, BLOCK)
            o0 = pl.multiple_of(g * BLOCK, BLOCK)
            held[:, pl.ds(o0, BLOCK)] = arrived[pl.ds(r0, width), pl.ds(c0, BLOCK)].astype(F32)
        put_out(at).start()
        return carry

    total = jnp.zeros((1, width), F32)
    for j in range(STEPS):
        held[:, j * BLOCK : (j + 1) * BLOCK] = owns[j][...]
        total = total + squares[j][...]
    variance[...] = total * (1.0 / (STEPS * BLOCK))
    put_out(0).start()
    lax.fori_loop(1, blocks // group, place_group, 0)

    def drain(at, carry):
        put_out(at).wait()
        return carry

    lax.fori_loop(0, blocks // group, drain, 0)


def call(kernel, outs, in_specs, out_specs, scalars=0, scratch=(), flops=0):
    return pl.pallas_call(
        kernel,
        grid_spec=pltpu.PrefetchScalarGridSpec(
            num_scalar_prefetch=scalars,
            in_specs=in_specs,
            out_specs=out_specs,
            scratch_shapes=scratch,
        ),
        out_shape=outs,
        compiler_params=pltpu.CompilerParams(vmem_limit_bytes=VMEM_LIMIT),
        cost_estimate=pl.CostEstimate(flops=flops, bytes_accessed=0, transcendentals=0),
    )


def hop(value, count, even, odd):
    return lax.ppermute(
        value, "row", [(i, i ^ (odd if i % 2 else even)) for i in range(count)]
    )


def orders(count):
    masks = [1 << bit for bit in range(1, count.bit_length() - 1)]
    masks = masks[:1] + masks[-1:] + masks[1:-1]
    return list(zip(masks, masks))


def spread(value, count, needed, beside, late):
    done = after = []
    steps = orders(count)
    for at, (even, odd) in enumerate(steps):
        arrived = hop(value, count, even, odd)
        if at == len(steps) - 1:
            value, arrived, *after = lax.optimization_barrier((value, arrived, *after))
            return (value, arrived), done, after
        value = value + arrived
        if at == 0 and beside:
            value, needed = lax.optimization_barrier((value, needed))
            done = beside(needed)
        elif at == 1:
            value, done, needed = lax.optimization_barrier((value, done, needed))
            after = late(needed)


def on_device(factor_panel, pivots, right_sides, block_home):
    slots = factor_panel.shape[0] // BLOCK
    held_rows, columns = right_sides.shape
    count = lax.axis_size("row")
    width = columns // count
    blocks = block_home.shape[0]
    total = blocks * BLOCK
    shape = jax.ShapeDtypeStruct
    half = shape((BLOCK, columns // 2), BF)
    vmem = pl.BlockSpec(memory_space=pltpu.VMEM)
    hbm = pl.BlockSpec(memory_space=pltpu.HBM)
    pivot_row = pivots.reshape(1, PANEL)
    keep, send = call(
        functools.partial(first_kernel, slots, width),
        [half, half],
        [hbm] * 4,
        [vmem] * 2,
        scratch=(
            pltpu.SMEM((blocks,), jnp.int32),
            pltpu.VMEM((held_rows, BLOCK), BF),
            pltpu.VMEM((1, PANEL), F32),
            pltpu.VMEM((held_rows, columns), F32),
            pltpu.SemaphoreType.DMA((4,)),
        ),
    )(*(
        pltpu.with_memory_space_constraint(value, pltpu.HBM)
        for value in (block_home, factor_panel, pivot_row, right_sides)
    ))
    mine = keep + hop(send, count, 1, 1)

    def ready(k, there, solved):
        return call(
            functools.partial(ready_kernel, k, slots, width),
            [
                shape((2 * BLOCK, BLOCK), BF),
                shape((BLOCK, HALF), BF),
                shape((BLOCK, columns // 2), F32),
            ],
            [vmem] * (4 + k),
            [vmem] * 3,
            scalars=1,
            flops=5 * 10**8,
        )(block_home, factor_panel, there[0], pivot_row, right_sides, there[1], *solved)

    mine, rows_sent, factor_sent = lax.optimization_barrier(
        (keep + hop(send, count, 1, 1), right_sides, factor_panel)
    )
    shared = (hop(factor_sent, count, 1, 1), hop(rows_sent, count, 1, 1))
    terms, _, prepared = spread(mine, count, shared, None, lambda there: ready(1, there, []))
    solved = []
    rest = [right_sides, shared[1]]
    owns, squares = [], []
    own_shapes = [shape((width, BLOCK), F32), shape((1, width), F32)]
    for k in range(1, STEPS):
        piece, whole = call(
            functools.partial(step_kernel, k, slots), [half, half], [vmem] * 5, [vmem] * 2, scalars=1
        )(block_home, *prepared, *terms)
        update = call(
            functools.partial(early_kernel, k - 1, width),
            [shape((2 * held_rows, columns // 2), F32), *own_shapes],
            [vmem] * (3 + len(rest)),
            [vmem] * 3,
            flops=2 * held_rows * columns * BLOCK,
        )
        terms, (left, own, square), prepared = spread(
            piece,
            count,
            whole,
            lambda gated: update(factor_panel, shared[0], *rest, gated),
            lambda gated: ready(k + 1, shared, [*solved, gated]) if k + 1 < STEPS else [],
        )
        rest = [left]
        solved.append(whole)
        owns.append(own)
        squares.append(square)
    turned, own, square = call(
        functools.partial(last_kernel, width),
        [shape((columns // 2, 2 * held_rows), BF), *own_shapes],
        [vmem] * 5,
        [vmem] * 3,
    )(factor_panel, shared[0], *rest, *terms)
    owns.append(own)
    squares.append(square)
    arrived = lax.all_to_all(
        turned,
        "row",
        split_axis=0,
        concat_axis=0,
        tiled=True,
        axis_index_groups=[list(range(core, count, 2)) for core in range(2)],
    )
    out, variance = call(
        functools.partial(order_kernel, slots, width),
        [shape((width, total), F32), shape((1, width), F32)],
        [vmem] * (1 + 2 * STEPS),
        [hbm, vmem],
        scalars=1,
        scratch=(pltpu.VMEM((width, total), F32), pltpu.SemaphoreType.DMA((blocks // STEPS,))),
    )(block_home, arrived, *owns, *squares)
    return out.T, variance[0]


def solution(mesh):
    in_specs = (P(("groups", "row"), None), P("groups"), P(("groups", "row"), None), P())
    out_specs = (P("groups", "row"), P(("groups", "row")))
    return jax.shard_map(
        on_device, mesh=mesh, in_specs=in_specs, out_specs=out_specs, check_vma=False
    )
```

```python
import functools

import jax
import jax.numpy as jnp
from jax import lax
from jax.experimental import pallas as pl
from jax.experimental.pallas import tpu as pltpu
from jax.sharding import PartitionSpec as P

BLOCK = 512
HALF = 256
STEPS = 4
START = 16
PANEL = 2048
BF = jnp.bfloat16
F32 = jnp.float32
VMEM_LIMIT = 24 * 1024 * 1024


def mm(a, b):
    return jnp.dot(a, b, preferred_element_type=F32)


def mm_nt(a, b):
    return lax.dot_general(a, b, (((1,), (1,)), ((), ())), preferred_element_type=F32)


def parts(value):
    high = value.astype(BF)
    return high, (value - high.astype(F32)).astype(BF)


def mm3(a_high, a_low, b):
    b_high, b_low = parts(b)
    rows, width = a_high.shape[0], b.shape[1]
    if width <= 128:
        both = mm(jnp.concatenate([a_high, a_low]), jnp.concatenate([b_high, b_low], axis=1))
        return both[:rows, :width] + (both[:rows, width:] + both[rows:, :width])
    return mm(a_high, b_high) + (mm(a_high, b_low) + mm(a_low, b_high))


def mm2(a, b):
    b_high, b_low = parts(b)
    width = b.shape[1]
    if width <= 128:
        both = mm(a, jnp.concatenate([b_high, b_low], axis=1))
        return both[:, :width] + both[:, width:]
    return mm(a, b_high) + mm(a, b_low)


def odd_rows(value, size):
    picked = [value[at : at + size] for at in range(size, value.shape[0], 2 * size)]
    return picked[0] if len(picked) == 1 else jnp.concatenate(picked, axis=0)


def put_odd_rows(value, odd, size):
    pieces = []
    for at in range(0, value.shape[0], size):
        turn = at // size
        pieces.append(
            value[at : at + size] if turn % 2 == 0 else odd[turn // 2 * size : (turn // 2 + 1) * size]
        )
    return jnp.concatenate(pieces, axis=0)


def double(tile, inverse, halves, size, apart, lower):
    high, low = halves
    width = tile.shape[1]
    link = jnp.where((lax.shift_right_logical(apart, size.bit_length() - 1) == 1) & lower, tile, 0.0)
    link = link.astype(BF)
    packed = size >= 16
    if packed:
        link = odd_rows(link, size)
        left_high, left_low = odd_rows(high, size), odd_rows(low, size)
    else:
        left_high, left_low = high, low
    if width <= 128:
        both = mm(link, jnp.concatenate([high, low], axis=1))
        inner = both[:, :width] + both[:, width:]
    else:
        inner = mm(link, high) + mm(link, low)
    if packed:
        zero = jnp.zeros((size, width), F32)
        pieces = []
        for at in range(inner.shape[0] // size):
            pieces += [zero, inner[at * size : (at + 1) * size]]
        inner = jnp.concatenate(pieces, axis=0)
    inner_high, inner_low = parts(inner)
    if width <= 128:
        rows = left_high.shape[0]
        both = mm(
            jnp.concatenate([left_high, left_low], axis=0),
            jnp.concatenate([inner_high, inner_low], axis=1),
        )
        change = both[:rows, :width] + (both[:rows, width:] + both[rows:, :width])
    else:
        change = mm(left_high, inner_high) + (mm(left_high, inner_low) + mm(left_low, inner_high))
    if packed:
        inverse = put_odd_rows(inverse, odd_rows(inverse, size) - change, size)
    else:
        inverse = inverse - change
    return inverse, parts(inverse)


def index_maps(shape):
    row = lax.broadcasted_iota(jnp.int32, shape, 0)
    col = lax.broadcasted_iota(jnp.int32, shape, 1)
    return row == col, row ^ col, row > col


def start_blocks(piece, across, down):
    width = piece.shape[1]
    shape = (START, width)
    lane = lax.broadcasted_iota(jnp.int32, shape, 1)
    row = lax.broadcasted_iota(jnp.int32, shape, 0)
    block, col = lax.shift_right_logical(lane, START.bit_length() - 1), lane & (START - 1)
    held = jnp.zeros(shape, F32)
    for b in range(width // START):
        held = jnp.where(block == b, piece[START * b : START * (b + 1)], held)
    held = jnp.where(row > col, held, 0.0) * across
    unit = jnp.where(row == col, 1.0, 0.0).astype(F32)
    for j in range(START - 1):
        factor = jnp.where(col == j, held, 0.0)
        if j:
            factor = pltpu.roll(factor, width - j, 1)
        shift = 1
        while shift < START:
            factor = factor + pltpu.roll(factor, shift, 1)
            shift *= 2
        unit = unit - factor * unit[j : j + 1]
    spread_out = [jnp.where(block == b, unit, 0.0) for b in range(width // START)]
    return jnp.concatenate(spread_out, axis=0) * down


def invert(tiles, pivot_rows):
    quarter = HALF // 2
    on, apart, lower = index_maps((quarter, quarter))
    small, values = [], []
    for tile, pivot in zip(tiles, pivot_rows):
        for at in range(0, HALF, quarter):
            piece = tile[at : at + quarter, at : at + quarter].astype(F32)
            across = 1.0 / pivot[:, at : at + quarter]
            down = jnp.sum(jnp.where(on, across, 0.0), axis=1, keepdims=True)
            small.append(piece)
            values.append(start_blocks(piece, across, down))
    halves = [parts(value) for value in values]
    size = START
    while size < quarter:
        for at, piece in enumerate(small):
            values[at], halves[at] = double(piece, values[at], halves[at], size, apart, lower)
        size *= 2
    zero = jnp.zeros((quarter, quarter), F32)
    _, apart, lower = index_maps((HALF, HALF))
    result = []
    for at, tile in enumerate(tiles):
        value = jnp.concatenate(
            [
                jnp.concatenate([values[2 * at], zero], axis=1),
                jnp.concatenate([zero, values[2 * at + 1]], axis=1),
            ],
            axis=0,
        )
        result.append(double(tile.astype(F32), value, parts(value), quarter, apart, lower)[1])
    return result


def solve(tile_cross, inv, rows):
    top = mm3(*inv[0], rows[:HALF])
    bottom = mm3(*inv[1], rows[HALF:] - mm2(tile_cross, top))
    return top.astype(BF), bottom.astype(BF)


def pick_columns(columns, width, parity):
    shape = (columns, columns // 2)
    row = lax.broadcasted_iota(jnp.int32, shape, 0)
    col = lax.broadcasted_iota(jnp.int32, shape, 1)
    bits = width.bit_length() - 1
    group = lax.shift_right_logical(col, bits)
    wanted = (2 * group + parity) * width + (col & (width - 1))
    return jnp.where(row == wanted, 1.0, 0.0).astype(BF)


def picked(value, chosen):
    high = value.astype(BF)
    rest = value - high.astype(F32)
    middle, low = parts(rest)
    return mm(high, chosen) + (mm(middle, chosen) + mm(low, chosen))


def first_kernel(slots, width, home_ref, factor, pivots, rows, keep, send, home, tile, pivot, value, sems):
    me = lax.axis_index("row")
    fetch_home = pltpu.make_async_copy(home_ref, home, sems.at[0])
    fetch_pivot = pltpu.make_async_copy(pivots, pivot, sems.at[1])
    fetch_tile = pltpu.make_async_copy(factor.at[:, pl.ds(0, BLOCK)], tile, sems.at[2])
    fetch_rows = pltpu.make_async_copy(rows, value, sems.at[3])
    fetch_home.start()
    fetch_tile.start()
    fetch_pivot.start()
    fetch_rows.start()
    fetch_home.wait()
    owner = home[0] // slots == me
    r0 = pl.multiple_of(home[0] % slots * BLOCK, BLOCK)
    fetch_pivot.wait()
    fetch_tile.wait()
    fetch_rows.wait()

    @pl.when(owner)
    def _():
        pieces = [
            tile[pl.ds(r0 + h * HALF, HALF), h * HALF : (h + 1) * HALF] for h in range(2)
        ]
        inv = invert(pieces, [pivot[:, h * HALF : (h + 1) * HALF] for h in range(2)])
        cross = tile[pl.ds(r0 + HALF, HALF), :HALF]
        top, bottom = solve(cross, inv, value[pl.ds(r0, BLOCK), :])
        here = pick_columns(rows.shape[1], width, me % 2)
        there = pick_columns(rows.shape[1], width, 1 - me % 2)
        for at, part in enumerate((top, bottom)):
            span = slice(at * HALF, (at + 1) * HALF)
            keep[span, :] = mm(part, here).astype(BF)
            send[span, :] = mm(part, there).astype(BF)

    @pl.when(jnp.logical_not(owner))
    def _():
        keep[...] = jnp.zeros_like(keep)
        send[...] = jnp.zeros_like(send)


def ready_kernel(k, slots, width, home, factor, factor_there, pivots, rows, rows_there, *refs):
    solved, (weights, cross, start) = refs[: k - 1], refs[k - 1 :]
    me = lax.axis_index("row")
    r0 = pl.multiple_of(home[k] % slots * BLOCK, BLOCK)
    for there, (held, right) in enumerate(((factor, rows), (factor_there, rows_there))):

        @pl.when(home[k] // slots == (me ^ there))
        def _(held=held, right=right):
            spans = [slice(k * BLOCK + h * HALF, k * BLOCK + (h + 1) * HALF) for h in range(2)]
            pieces = [held[pl.ds(r0 + h * HALF, HALF), span] for h, span in enumerate(spans)]
            inv = invert(pieces, [pivots[:, span] for span in spans])
            chosen = pick_columns(right.shape[1], width, me % 2)
            value = picked(right[pl.ds(r0, BLOCK), :], chosen)
            for j in range(k - 1):
                value = value - mm(
                    held[pl.ds(r0, BLOCK), j * BLOCK : (j + 1) * BLOCK], solved[j][...]
                )
            for h, (high, low) in enumerate(inv):
                span = slice(h * HALF, (h + 1) * HALF)
                low_span = slice(BLOCK + h * HALF, BLOCK + (h + 1) * HALF)
                left = held[pl.ds(r0 + h * HALF, HALF), (k - 1) * BLOCK : k * BLOCK]
                weights[span, :], weights[low_span, :] = parts(mm(high, left) + mm(low, left))
                start[span, :] = mm3(high, low, value[span])
            high, low = inv[1]
            link = held[pl.ds(r0 + HALF, HALF), spans[0]]
            cross[:HALF, :], cross[HALF:, :] = parts(mm(high, link) + mm(low, link))


def step_kernel(k, slots, home, weights, cross, start, before, arrived, piece, whole):
    me = lax.axis_index("row")
    previous = before[...] + arrived[...]
    whole[...] = previous
    owner = home[k] // (2 * slots) == me // 2

    @pl.when(owner)
    def _():
        both = mm(weights[...], previous)
        value = start[...] - (both[:BLOCK] + both[BLOCK:])
        top = value[:HALF]
        piece[:HALF, :] = top.astype(BF)
        piece[HALF:, :] = (value[HALF:] - mm3(cross[:HALF, :], cross[HALF:, :], top)).astype(BF)

    @pl.when(jnp.logical_not(owner))
    def _():
        piece[...] = jnp.zeros_like(piece)


def columns_of(half, at, width):
    shape = (width, half.shape[1])
    pick = (
        lax.broadcasted_iota(jnp.int32, shape, 1)
        == lax.broadcasted_iota(jnp.int32, shape, 0) + at * width
    ).astype(F32).astype(BF)
    return mm_nt(pick, half)


def row_of_squares(value):
    high, low = parts(value * value)
    ones = jnp.ones((8, value.shape[1]), BF)
    return (mm_nt(ones, high) + mm_nt(ones, low))[:1]


def early_kernel(k, width, factor, factor_there, *refs):
    before, (solved, rest, own, squares) = refs[:-4], refs[-4:]
    me = lax.axis_index("row")
    full = solved[...]
    held_rows = factor.shape[0]
    for at, held in enumerate((factor, factor_there)):
        for r0 in range(0, held_rows, HALF):
            span = slice(at * held_rows + r0, at * held_rows + r0 + HALF)
            here = slice(r0, r0 + HALF)
            if k == 0:
                right = before[at]
                value = picked(right[here, :], pick_columns(right.shape[1], width, me % 2))
            else:
                value = before[0][span, :]
            rest[span, :] = value - mm(held[here, k * BLOCK : (k + 1) * BLOCK], full)
    own_columns(me // 2, width, full, own, squares)


def own_columns(at, width, full, own, squares):
    value = columns_of(full, at, width)
    own[...] = value
    squares[...] = row_of_squares(value)


def last_kernel(width, factor, factor_there, rest, before, arrived, out, own, squares):
    me = lax.axis_index("row")
    full = before[...] + arrived[...]
    columns = rest.shape[1]
    size = min(HALF, columns)
    on, _, _ = index_maps((size, size))
    eye = on.astype(F32).astype(BF)
    held_rows = factor.shape[0]
    for at, held in enumerate((factor, factor_there)):
        place = pl.multiple_of((me % 2 ^ at) * held_rows, held_rows)
        for r0 in range(0, held_rows, HALF):
            value = rest[at * held_rows + r0 : at * held_rows + r0 + HALF, :]
            value = value - mm(held[r0 : r0 + HALF, (STEPS - 1) * BLOCK :], full)
            value = value.astype(BF)
            for c in range(0, columns, size):
                out[c : c + size, pl.ds(place + r0, HALF)] = mm_nt(
                    eye, value[:, c : c + size]
                ).astype(BF)
    own_columns(me // 2, width, full, own, squares)


def order_kernel(slots, width, home, arrived, *refs):
    owns, squares = refs[:STEPS], refs[STEPS : 2 * STEPS]
    out, variance, held, sems = refs[2 * STEPS :]
    blocks = held.shape[1] // BLOCK
    group = STEPS

    def put_out(at):
        span = pl.ds(pl.multiple_of(at * group * BLOCK, BLOCK), group * BLOCK)
        return pltpu.make_async_copy(held.at[:, span], out.at[:, span], sems.at[at])

    def place_group(at, carry):
        for turn_at in range(group):
            g = at * group + turn_at
            spot = home[g]
            r0 = pl.multiple_of(spot // (2 * slots) * width, width)
            c0 = pl.multiple_of(spot % (2 * slots) * BLOCK, BLOCK)
            o0 = pl.multiple_of(g * BLOCK, BLOCK)
            held[:, pl.ds(o0, BLOCK)] = arrived[pl.ds(r0, width), pl.ds(c0, BLOCK)].astype(F32)
        put_out(at).start()
        return carry

    total = jnp.zeros((1, width), F32)
    for j in range(STEPS):
        held[:, j * BLOCK : (j + 1) * BLOCK] = owns[j][...]
        total = total + squares[j][...]
    variance[...] = total * (1.0 / (STEPS * BLOCK))
    put_out(0).start()
    lax.fori_loop(1, blocks // group, place_group, 0)

    def drain(at, carry):
        put_out(at).wait()
        return carry

    lax.fori_loop(0, blocks // group, drain, 0)


def call(kernel, outs, in_specs, out_specs, scalars=0, scratch=(), flops=0):
    return pl.pallas_call(
        kernel,
        grid_spec=pltpu.PrefetchScalarGridSpec(
            num_scalar_prefetch=scalars,
            in_specs=in_specs,
            out_specs=out_specs,
            scratch_shapes=scratch,
        ),
        out_shape=outs,
        compiler_params=pltpu.CompilerParams(vmem_limit_bytes=VMEM_LIMIT),
        cost_estimate=pl.CostEstimate(flops=flops, bytes_accessed=0, transcendentals=0),
    )


def hop(value, count, even, odd):
    return lax.ppermute(
        value, "row", [(i, i ^ (odd if i % 2 else even)) for i in range(count)]
    )


def orders(count):
    masks = [1 << bit for bit in range(1, count.bit_length() - 1)]
    return [(mask, mask) for mask in reversed(masks)]


def spread(value, count, needed, beside, late):
    done = after = []
    steps = orders(count)
    for at, (even, odd) in enumerate(steps):
        arrived = hop(value, count, even, odd)
        if at == len(steps) - 1:
            value, arrived, *after = lax.optimization_barrier((value, arrived, *after))
            return (value, arrived), done, after
        value = value + arrived
        if at == 0 and beside:
            value, needed = lax.optimization_barrier((value, needed))
            done = beside(needed)
        elif at == 1:
            value, done, needed = lax.optimization_barrier((value, done, needed))
            after = late(needed)


def on_device(factor_panel, pivots, right_sides, block_home):
    slots = factor_panel.shape[0] // BLOCK
    held_rows, columns = right_sides.shape
    count = lax.axis_size("row")
    width = columns // count
    blocks = block_home.shape[0]
    total = blocks * BLOCK
    shape = jax.ShapeDtypeStruct
    half = shape((BLOCK, columns // 2), BF)
    vmem = pl.BlockSpec(memory_space=pltpu.VMEM)
    hbm = pl.BlockSpec(memory_space=pltpu.HBM)
    pivot_row = pivots.reshape(1, PANEL)
    keep, send = call(
        functools.partial(first_kernel, slots, width),
        [half, half],
        [hbm] * 4,
        [vmem] * 2,
        scratch=(
            pltpu.SMEM((blocks,), jnp.int32),
            pltpu.VMEM((held_rows, BLOCK), BF),
            pltpu.VMEM((1, PANEL), F32),
            pltpu.VMEM((held_rows, columns), F32),
            pltpu.SemaphoreType.DMA((4,)),
        ),
    )(*(
        pltpu.with_memory_space_constraint(value, pltpu.HBM)
        for value in (block_home, factor_panel, pivot_row, right_sides)
    ))
    mine = keep + hop(send, count, 1, 1)

    def ready(k, there, solved):
        return call(
            functools.partial(ready_kernel, k, slots, width),
            [
                shape((2 * BLOCK, BLOCK), BF),
                shape((BLOCK, HALF), BF),
                shape((BLOCK, columns // 2), F32),
            ],
            [vmem] * (4 + k),
            [vmem] * 3,
            scalars=1,
            flops=5 * 10**8,
        )(block_home, factor_panel, there[0], pivot_row, right_sides, there[1], *solved)

    mine, rows_sent, factor_sent = lax.optimization_barrier(
        (keep + hop(send, count, 1, 1), right_sides, factor_panel)
    )
    shared = (hop(factor_sent, count, 1, 1), hop(rows_sent, count, 1, 1))
    terms, _, prepared = spread(mine, count, shared, None, lambda there: ready(1, there, []))
    solved = []
    rest = [right_sides, shared[1]]
    owns, squares = [], []
    own_shapes = [shape((width, BLOCK), F32), shape((1, width), F32)]
    for k in range(1, STEPS):
        piece, whole = call(
            functools.partial(step_kernel, k, slots), [half, half], [vmem] * 5, [vmem] * 2, scalars=1
        )(block_home, *prepared, *terms)
        update = call(
            functools.partial(early_kernel, k - 1, width),
            [shape((2 * held_rows, columns // 2), F32), *own_shapes],
            [vmem] * (3 + len(rest)),
            [vmem] * 3,
            flops=2 * held_rows * columns * BLOCK,
        )
        terms, (left, own, square), prepared = spread(
            piece,
            count,
            whole,
            lambda gated: update(factor_panel, shared[0], *rest, gated),
            lambda gated: ready(k + 1, shared, [*solved, gated]) if k + 1 < STEPS else [],
        )
        rest = [left]
        solved.append(whole)
        owns.append(own)
        squares.append(square)
    turned, own, square = call(
        functools.partial(last_kernel, width),
        [shape((columns // 2, 2 * held_rows), BF), *own_shapes],
        [vmem] * 5,
        [vmem] * 3,
    )(factor_panel, shared[0], *rest, *terms)
    owns.append(own)
    squares.append(square)
    arrived = lax.all_to_all(
        turned,
        "row",
        split_axis=0,
        concat_axis=0,
        tiled=True,
        axis_index_groups=[list(range(core, count, 2)) for core in range(2)],
    )
    out, variance = call(
        functools.partial(order_kernel, slots, width),
        [shape((width, total), F32), shape((1, width), F32)],
        [vmem] * (1 + 2 * STEPS),
        [hbm, vmem],
        scalars=1,
        scratch=(pltpu.VMEM((width, total), F32), pltpu.SemaphoreType.DMA((blocks // STEPS,))),
    )(block_home, arrived, *owns, *squares)
    return out.T, variance[0]


def solution(mesh):
    in_specs = (P(("groups", "row"), None), P("groups"), P(("groups", "row"), None), P())
    out_specs = (P("groups", "row"), P(("groups", "row")))
    return jax.shard_map(
        on_device, mesh=mesh, in_specs=in_specs, out_specs=out_specs, check_vma=False
    )
```

```python
import functools

import jax
import jax.numpy as jnp
from jax import lax
from jax.experimental import pallas as pl
from jax.experimental.pallas import tpu as pltpu
from jax.sharding import PartitionSpec as P

BLOCK = 512
HALF = 256
STEPS = 4
START = 16
PANEL = 2048
BF = jnp.bfloat16
F32 = jnp.float32
VMEM_LIMIT = 24 * 1024 * 1024


def mm(a, b):
    return jnp.dot(a, b, preferred_element_type=F32)


def mm_nt(a, b):
    return lax.dot_general(a, b, (((1,), (1,)), ((), ())), preferred_element_type=F32)


def parts(value):
    high = value.astype(BF)
    return high, (value - high.astype(F32)).astype(BF)


def mm3(a_high, a_low, b):
    b_high, b_low = parts(b)
    rows, width = a_high.shape[0], b.shape[1]
    if width <= 128:
        both = mm(jnp.concatenate([a_high, a_low]), jnp.concatenate([b_high, b_low], axis=1))
        return both[:rows, :width] + (both[:rows, width:] + both[rows:, :width])
    return mm(a_high, b_high) + (mm(a_high, b_low) + mm(a_low, b_high))


def mm2(a, b):
    b_high, b_low = parts(b)
    width = b.shape[1]
    if width <= 128:
        both = mm(a, jnp.concatenate([b_high, b_low], axis=1))
        return both[:, :width] + both[:, width:]
    return mm(a, b_high) + mm(a, b_low)


def odd_rows(value, size):
    picked = [value[at : at + size] for at in range(size, value.shape[0], 2 * size)]
    return picked[0] if len(picked) == 1 else jnp.concatenate(picked, axis=0)


def put_odd_rows(value, odd, size):
    pieces = []
    for at in range(0, value.shape[0], size):
        turn = at // size
        pieces.append(
            value[at : at + size] if turn % 2 == 0 else odd[turn // 2 * size : (turn // 2 + 1) * size]
        )
    return jnp.concatenate(pieces, axis=0)


def double(tile, inverse, halves, size, apart, lower):
    high, low = halves
    width = tile.shape[1]
    link = jnp.where((lax.shift_right_logical(apart, size.bit_length() - 1) == 1) & lower, tile, 0.0)
    link = link.astype(BF)
    packed = size >= 16
    if packed:
        link = odd_rows(link, size)
        left_high, left_low = odd_rows(high, size), odd_rows(low, size)
    else:
        left_high, left_low = high, low
    if width <= 128:
        both = mm(link, jnp.concatenate([high, low], axis=1))
        inner = both[:, :width] + both[:, width:]
    else:
        inner = mm(link, high) + mm(link, low)
    if packed:
        zero = jnp.zeros((size, width), F32)
        pieces = []
        for at in range(inner.shape[0] // size):
            pieces += [zero, inner[at * size : (at + 1) * size]]
        inner = jnp.concatenate(pieces, axis=0)
    inner_high, inner_low = parts(inner)
    if width <= 128:
        rows = left_high.shape[0]
        both = mm(
            jnp.concatenate([left_high, left_low], axis=0),
            jnp.concatenate([inner_high, inner_low], axis=1),
        )
        change = both[:rows, :width] + (both[:rows, width:] + both[rows:, :width])
    else:
        change = mm(left_high, inner_high) + (mm(left_high, inner_low) + mm(left_low, inner_high))
    if packed:
        inverse = put_odd_rows(inverse, odd_rows(inverse, size) - change, size)
    else:
        inverse = inverse - change
    return inverse, parts(inverse)


def index_maps(shape):
    row = lax.broadcasted_iota(jnp.int32, shape, 0)
    col = lax.broadcasted_iota(jnp.int32, shape, 1)
    return row == col, row ^ col, row > col


def start_blocks(piece, across, down):
    width = piece.shape[1]
    shape = (START, width)
    lane = lax.broadcasted_iota(jnp.int32, shape, 1)
    row = lax.broadcasted_iota(jnp.int32, shape, 0)
    block, col = lax.shift_right_logical(lane, START.bit_length() - 1), lane & (START - 1)
    held = jnp.zeros(shape, F32)
    for b in range(width // START):
        held = jnp.where(block == b, piece[START * b : START * (b + 1)], held)
    held = jnp.where(row > col, held, 0.0) * across
    unit = jnp.where(row == col, 1.0, 0.0).astype(F32)
    for j in range(START - 1):
        factor = jnp.where(col == j, held, 0.0)
        if j:
            factor = pltpu.roll(factor, width - j, 1)
        shift = 1
        while shift < START:
            factor = factor + pltpu.roll(factor, shift, 1)
            shift *= 2
        unit = unit - factor * unit[j : j + 1]
    spread_out = [jnp.where(block == b, unit, 0.0) for b in range(width // START)]
    return jnp.concatenate(spread_out, axis=0) * down


def invert(tiles, pivot_rows):
    quarter = HALF // 2
    on, apart, lower = index_maps((quarter, quarter))
    small, values = [], []
    for tile, pivot in zip(tiles, pivot_rows):
        for at in range(0, HALF, quarter):
            piece = tile[at : at + quarter, at : at + quarter].astype(F32)
            across = 1.0 / pivot[:, at : at + quarter]
            down = jnp.sum(jnp.where(on, across, 0.0), axis=1, keepdims=True)
            small.append(piece)
            values.append(start_blocks(piece, across, down))
    halves = [parts(value) for value in values]
    size = START
    while size < quarter:
        for at, piece in enumerate(small):
            values[at], halves[at] = double(piece, values[at], halves[at], size, apart, lower)
        size *= 2
    zero = jnp.zeros((quarter, quarter), F32)
    _, apart, lower = index_maps((HALF, HALF))
    result = []
    for at, tile in enumerate(tiles):
        value = jnp.concatenate(
            [
                jnp.concatenate([values[2 * at], zero], axis=1),
                jnp.concatenate([zero, values[2 * at + 1]], axis=1),
            ],
            axis=0,
        )
        result.append(double(tile.astype(F32), value, parts(value), quarter, apart, lower)[1])
    return result


def solve(tile_cross, inv, rows):
    top = mm3(*inv[0], rows[:HALF])
    bottom = mm3(*inv[1], rows[HALF:] - mm2(tile_cross, top))
    return top.astype(BF), bottom.astype(BF)


def pick_columns(columns, width, parity):
    shape = (columns, columns // 2)
    row = lax.broadcasted_iota(jnp.int32, shape, 0)
    col = lax.broadcasted_iota(jnp.int32, shape, 1)
    bits = width.bit_length() - 1
    group = lax.shift_right_logical(col, bits)
    wanted = (2 * group + parity) * width + (col & (width - 1))
    return jnp.where(row == wanted, 1.0, 0.0).astype(BF)


def picked(value, chosen):
    high = value.astype(BF)
    rest = value - high.astype(F32)
    middle, low = parts(rest)
    return mm(high, chosen) + (mm(middle, chosen) + mm(low, chosen))


def first_kernel(slots, width, home_ref, factor, pivots, rows, keep, send, home, tile, pivot, value, sems):
    me = lax.axis_index("row")
    fetch_home = pltpu.make_async_copy(home_ref, home, sems.at[0])
    fetch_pivot = pltpu.make_async_copy(pivots, pivot, sems.at[1])
    fetch_tile = pltpu.make_async_copy(factor.at[:, pl.ds(0, BLOCK)], tile, sems.at[2])
    fetch_rows = pltpu.make_async_copy(rows, value, sems.at[3])
    fetch_home.start()
    fetch_tile.start()
    fetch_pivot.start()
    fetch_rows.start()
    fetch_home.wait()
    owner = home[0] // slots == me
    r0 = pl.multiple_of(home[0] % slots * BLOCK, BLOCK)
    fetch_pivot.wait()
    fetch_tile.wait()
    fetch_rows.wait()

    @pl.when(owner)
    def _():
        pieces = [
            tile[pl.ds(r0 + h * HALF, HALF), h * HALF : (h + 1) * HALF] for h in range(2)
        ]
        inv = invert(pieces, [pivot[:, h * HALF : (h + 1) * HALF] for h in range(2)])
        cross = tile[pl.ds(r0 + HALF, HALF), :HALF]
        top, bottom = solve(cross, inv, value[pl.ds(r0, BLOCK), :])
        here = pick_columns(rows.shape[1], width, me % 2)
        there = pick_columns(rows.shape[1], width, 1 - me % 2)
        for at, part in enumerate((top, bottom)):
            span = slice(at * HALF, (at + 1) * HALF)
            keep[span, :] = mm(part, here).astype(BF)
            send[span, :] = mm(part, there).astype(BF)

    @pl.when(jnp.logical_not(owner))
    def _():
        keep[...] = jnp.zeros_like(keep)
        send[...] = jnp.zeros_like(send)


def ready_kernel(k, slots, width, home, factor, factor_there, pivots, rows, rows_there, *refs):
    solved, (weights, cross, start) = refs[: k - 1], refs[k - 1 :]
    me = lax.axis_index("row")
    r0 = pl.multiple_of(home[k] % slots * BLOCK, BLOCK)
    for there, (held, right) in enumerate(((factor, rows), (factor_there, rows_there))):

        @pl.when(home[k] // slots == (me ^ there))
        def _(held=held, right=right):
            spans = [slice(k * BLOCK + h * HALF, k * BLOCK + (h + 1) * HALF) for h in range(2)]
            pieces = [held[pl.ds(r0 + h * HALF, HALF), span] for h, span in enumerate(spans)]
            inv = invert(pieces, [pivots[:, span] for span in spans])
            chosen = pick_columns(right.shape[1], width, me % 2)
            value = picked(right[pl.ds(r0, BLOCK), :], chosen)
            for j in range(k - 1):
                value = value - mm(
                    held[pl.ds(r0, BLOCK), j * BLOCK : (j + 1) * BLOCK], solved[j][...]
                )
            for h, (high, low) in enumerate(inv):
                span = slice(h * HALF, (h + 1) * HALF)
                low_span = slice(BLOCK + h * HALF, BLOCK + (h + 1) * HALF)
                left = held[pl.ds(r0 + h * HALF, HALF), (k - 1) * BLOCK : k * BLOCK]
                weights[span, :], weights[low_span, :] = parts(mm(high, left) + mm(low, left))
                start[span, :] = mm3(high, low, value[span])
            high, low = inv[1]
            link = held[pl.ds(r0 + HALF, HALF), spans[0]]
            cross[:HALF, :], cross[HALF:, :] = parts(mm(high, link) + mm(low, link))


def step_kernel(k, slots, home, weights, cross, start, before, arrived, piece, whole):
    me = lax.axis_index("row")
    previous = before[...] + arrived[...]
    whole[...] = previous
    owner = home[k] // (2 * slots) == me // 2

    @pl.when(owner)
    def _():
        both = mm(weights[...], previous)
        value = start[...] - (both[:BLOCK] + both[BLOCK:])
        top = value[:HALF]
        piece[:HALF, :] = top.astype(BF)
        piece[HALF:, :] = (value[HALF:] - mm3(cross[:HALF, :], cross[HALF:, :], top)).astype(BF)

    @pl.when(jnp.logical_not(owner))
    def _():
        piece[...] = jnp.zeros_like(piece)


def columns_of(half, at, width):
    shape = (width, half.shape[1])
    pick = (
        lax.broadcasted_iota(jnp.int32, shape, 1)
        == lax.broadcasted_iota(jnp.int32, shape, 0) + at * width
    ).astype(F32).astype(BF)
    return mm_nt(pick, half)


def row_of_squares(value):
    high, low = parts(value * value)
    ones = jnp.ones((8, value.shape[1]), BF)
    return (mm_nt(ones, high) + mm_nt(ones, low))[:1]


def early_kernel(k, width, factor, factor_there, *refs):
    before, (solved, rest, own, squares) = refs[:-4], refs[-4:]
    me = lax.axis_index("row")
    full = solved[...]
    held_rows = factor.shape[0]
    for at, held in enumerate((factor, factor_there)):
        for r0 in range(0, held_rows, HALF):
            span = slice(at * held_rows + r0, at * held_rows + r0 + HALF)
            here = slice(r0, r0 + HALF)
            if k == 0:
                right = before[at]
                value = picked(right[here, :], pick_columns(right.shape[1], width, me % 2))
            else:
                value = before[0][span, :]
            rest[span, :] = value - mm(held[here, k * BLOCK : (k + 1) * BLOCK], full)
    own_columns(me // 2, width, full, own, squares)


def own_columns(at, width, full, own, squares):
    value = columns_of(full, at, width)
    own[...] = value
    squares[...] = row_of_squares(value)


def last_kernel(width, factor, factor_there, rest, before, arrived, out, own, squares):
    me = lax.axis_index("row")
    full = before[...] + arrived[...]
    columns = rest.shape[1]
    size = min(HALF, columns)
    on, _, _ = index_maps((size, size))
    eye = on.astype(F32).astype(BF)
    held_rows = factor.shape[0]
    for at, held in enumerate((factor, factor_there)):
        place = pl.multiple_of((me % 2 ^ at) * held_rows, held_rows)
        for r0 in range(0, held_rows, HALF):
            value = rest[at * held_rows + r0 : at * held_rows + r0 + HALF, :]
            value = value - mm(held[r0 : r0 + HALF, (STEPS - 1) * BLOCK :], full)
            value = value.astype(BF)
            for c in range(0, columns, size):
                out[c : c + size, pl.ds(place + r0, HALF)] = mm_nt(
                    eye, value[:, c : c + size]
                ).astype(BF)
    own_columns(me // 2, width, full, own, squares)


def order_kernel(slots, width, home, arrived, *refs):
    owns, squares = refs[:STEPS], refs[STEPS : 2 * STEPS]
    out, variance, held, sems = refs[2 * STEPS :]
    blocks = held.shape[1] // BLOCK
    group = STEPS

    def put_out(at):
        span = pl.ds(pl.multiple_of(at * group * BLOCK, BLOCK), group * BLOCK)
        return pltpu.make_async_copy(held.at[:, span], out.at[:, span], sems.at[at])

    def place_group(at, carry):
        for turn_at in range(group):
            g = at * group + turn_at
            spot = home[g]
            r0 = pl.multiple_of(spot // (2 * slots) * width, width)
            c0 = pl.multiple_of(spot % (2 * slots) * BLOCK, BLOCK)
            o0 = pl.multiple_of(g * BLOCK, BLOCK)
            held[:, pl.ds(o0, BLOCK)] = arrived[pl.ds(r0, width), pl.ds(c0, BLOCK)].astype(F32)
        put_out(at).start()
        return carry

    total = jnp.zeros((1, width), F32)
    for j in range(STEPS):
        held[:, j * BLOCK : (j + 1) * BLOCK] = owns[j][...]
        total = total + squares[j][...]
    variance[...] = total * (1.0 / (STEPS * BLOCK))
    put_out(0).start()
    lax.fori_loop(1, blocks // group, place_group, 0)

    def drain(at, carry):
        put_out(at).wait()
        return carry

    lax.fori_loop(0, blocks // group, drain, 0)


def call(kernel, outs, in_specs, out_specs, scalars=0, scratch=(), flops=0):
    return pl.pallas_call(
        kernel,
        grid_spec=pltpu.PrefetchScalarGridSpec(
            num_scalar_prefetch=scalars,
            in_specs=in_specs,
            out_specs=out_specs,
            scratch_shapes=scratch,
        ),
        out_shape=outs,
        compiler_params=pltpu.CompilerParams(vmem_limit_bytes=VMEM_LIMIT),
        cost_estimate=pl.CostEstimate(flops=flops, bytes_accessed=0, transcendentals=0),
    )


def hop(value, count, even, odd):
    return lax.ppermute(
        value, "row", [(i, i ^ (odd if i % 2 else even)) for i in range(count)]
    )


def orders(count):
    masks = [1 << bit for bit in range(1, count.bit_length() - 1)]
    return [(mask, mask) for mask in reversed(masks)]


def spread(value, count, needed, beside, late, early=()):
    done = after = []
    steps = orders(count)
    for at, (even, odd) in enumerate(steps):
        arrived = hop(value, count, even, odd)
        if at == len(steps) - 1:
            value, arrived, *after = lax.optimization_barrier((value, arrived, *after))
            return (value, arrived), done, after
        value = value + arrived
        if at == 0 and beside:
            value, needed, early = lax.optimization_barrier((value, needed, early))
            done = beside(needed)
        elif at == 1:
            value, done, needed = lax.optimization_barrier((value, done, needed))
            after = early if early else late(needed)


def on_device(factor_panel, pivots, right_sides, block_home):
    slots = factor_panel.shape[0] // BLOCK
    held_rows, columns = right_sides.shape
    count = lax.axis_size("row")
    width = columns // count
    blocks = block_home.shape[0]
    total = blocks * BLOCK
    shape = jax.ShapeDtypeStruct
    half = shape((BLOCK, columns // 2), BF)
    vmem = pl.BlockSpec(memory_space=pltpu.VMEM)
    hbm = pl.BlockSpec(memory_space=pltpu.HBM)
    pivot_row = pivots.reshape(1, PANEL)
    keep, send = call(
        functools.partial(first_kernel, slots, width),
        [half, half],
        [hbm] * 4,
        [vmem] * 2,
        scratch=(
            pltpu.SMEM((blocks,), jnp.int32),
            pltpu.VMEM((held_rows, BLOCK), BF),
            pltpu.VMEM((1, PANEL), F32),
            pltpu.VMEM((held_rows, columns), F32),
            pltpu.SemaphoreType.DMA((4,)),
        ),
    )(*(
        pltpu.with_memory_space_constraint(value, pltpu.HBM)
        for value in (block_home, factor_panel, pivot_row, right_sides)
    ))
    mine = keep + hop(send, count, 1, 1)

    def ready(k, there, solved):
        return call(
            functools.partial(ready_kernel, k, slots, width),
            [
                shape((2 * BLOCK, BLOCK), BF),
                shape((BLOCK, HALF), BF),
                shape((BLOCK, columns // 2), F32),
            ],
            [vmem] * (4 + k),
            [vmem] * 3,
            scalars=1,
            flops=5 * 10**8,
        )(block_home, factor_panel, there[0], pivot_row, right_sides, there[1], *solved)

    mine, rows_sent, factor_sent = lax.optimization_barrier(
        (keep + hop(send, count, 1, 1), right_sides, factor_panel)
    )
    shared = (hop(factor_sent, count, 1, 1), hop(rows_sent, count, 1, 1))
    terms, _, prepared = spread(mine, count, shared, None, lambda there: ready(1, there, []))
    solved = []
    rest = [right_sides, shared[1]]
    owns, squares = [], []
    own_shapes = [shape((width, BLOCK), F32), shape((1, width), F32)]
    for k in range(1, STEPS):
        piece, whole = call(
            functools.partial(step_kernel, k, slots), [half, half], [vmem] * 5, [vmem] * 2, scalars=1
        )(block_home, *prepared, *terms)
        update = call(
            functools.partial(early_kernel, k - 1, width),
            [shape((2 * held_rows, columns // 2), F32), *own_shapes],
            [vmem] * (3 + len(rest)),
            [vmem] * 3,
            flops=2 * held_rows * columns * BLOCK,
        )
        terms, (left, own, square), prepared = spread(
            piece,
            count,
            whole,
            lambda gated: update(factor_panel, shared[0], *rest, gated),
            lambda _: [],
            ready(k + 1, shared, [*solved, whole]) if k + 1 < STEPS else [],
        )
        rest = [left]
        solved.append(whole)
        owns.append(own)
        squares.append(square)
    turned, own, square = call(
        functools.partial(last_kernel, width),
        [shape((columns // 2, 2 * held_rows), BF), *own_shapes],
        [vmem] * 5,
        [vmem] * 3,
    )(factor_panel, shared[0], *rest, *terms)
    owns.append(own)
    squares.append(square)
    arrived = lax.all_to_all(
        turned,
        "row",
        split_axis=0,
        concat_axis=0,
        tiled=True,
        axis_index_groups=[list(range(core, count, 2)) for core in range(2)],
    )
    out, variance = call(
        functools.partial(order_kernel, slots, width),
        [shape((width, total), F32), shape((1, width), F32)],
        [vmem] * (1 + 2 * STEPS),
        [hbm, vmem],
        scalars=1,
        scratch=(pltpu.VMEM((width, total), F32), pltpu.SemaphoreType.DMA((blocks // STEPS,))),
    )(block_home, arrived, *owns, *squares)
    return out.T, variance[0]


def solution(mesh):
    in_specs = (P(("groups", "row"), None), P("groups"), P(("groups", "row"), None), P())
    out_specs = (P("groups", "row"), P(("groups", "row")))
    return jax.shard_map(
        on_device, mesh=mesh, in_specs=in_specs, out_specs=out_specs, check_vma=False
    )
```
